32 devices in a mesh: view: 2 (over y), tile: 16 (over z, x, core).
Axes of the slice: x: 2, y: 2, z: 4, core: 2. Of those that a mesh axis runs over, the one named last changes fastest.
Arguments:
- estimate: float32 [8, 512, 512], P(None, 'tile'), may hold values from 0.5 to 2
- observed: float32 [2, 8, 512, 512], P('view', None, 'tile'), may hold values from 0.2 to 4
- psf_taps: float32 [2, 3, 31], P('view'), may hold values from 0.05 to 1
Outputs:
- restored: float32 [8, 512, 512], P(None, 'tile')
The draws below stay inside these ranges and needn't reach their ends.
All inputs are finite; a program needn't handle non-finite values.
Results may differ from the reference program's by a relative error of at most 0.0001.
Values sent between devices are 32-bit elements; how exact they have to be, the bound alone decides.
No kernel may reach another device: no remote copies, remote signals or barrier semaphores. Data moves between devices by JAX's collectives and lax.ppermute only.
A program may use at most 64 MiB of HBM per device.

```python
import math
import jax
import jax.numpy as jnp
from jax import lax

DEPTH = 8
WIDTH = 512
TAPS = 31
ITERS = 2
HALF = 15
VIEWS = 2
NY = 512


def levels(key, dims, split, smallest, high):
    def one(axis_at, shards_of):
        draws = jax.random.uniform(jax.random.fold_in(jax.random.fold_in(key, 6), axis_at), (shards_of,), jnp.float32, smallest / len(split), high / len(split))
        return jnp.repeat(jnp.exp(draws), dims[axis_at] // shards_of).reshape((-1,) + (1,) * (len(dims) - axis_at - 1))

    factor_of = one(*split[0])
    for cut in split[1:]:
        factor_of = factor_of * one(*cut)
    return factor_of


def setup_inputs(seed: int = 0) -> dict:
    key_of = jax.random.split(jax.random.key(seed), 4)
    estimate = jnp.clip(0.5 + 1.5 * jax.random.uniform(key_of[0], (DEPTH, NY, WIDTH), jnp.float32) ** levels(key_of[0], (DEPTH, NY, WIDTH), ((1, 16),), -0.2, 0.2), 0.5, 2.0)
    observed = jnp.clip(0.2 + 3.8 * jax.random.uniform(key_of[1], (VIEWS, DEPTH, NY, WIDTH), jnp.float32) ** levels(key_of[1], (VIEWS, DEPTH, NY, WIDTH), ((0, 2), (2, 16)), -0.2, 0.2), 0.2, 4.0)
    psf_taps = jnp.clip(jnp.exp(math.log(1.0) - 2.9957323 * jax.random.uniform(key_of[2], (VIEWS, 3, TAPS), jnp.float32) ** levels(key_of[2], (VIEWS, 3, TAPS), ((0, 2),), -0.2, 0.2)), 0.05, 1.0)
    return {"estimate": estimate, "observed": observed, "psf_taps": psf_taps}


def conv_axis(field, taps, axis):
    count = field.shape[axis]
    widths = [(0, 0), (0, 0), (0, 0)]
    widths[axis] = (HALF, HALF)
    padded = jnp.pad(field, widths)
    total = jnp.zeros(field.shape, jnp.float32)
    for shift_at in range(TAPS):
        total = total + taps[shift_at] * lax.slice_in_dim(padded, shift_at, shift_at + count, axis=axis)
    return total


def separable(field, kernels):
    out = conv_axis(field, kernels[0], 0)
    out = conv_axis(out, kernels[1], 1)
    return conv_axis(out, kernels[2], 2)


def reference(estimate, observed, psf_taps):
    normed = psf_taps / jnp.sum(psf_taps, axis=2, keepdims=True)
    flipped = normed[:, :, ::-1]
    current = estimate
    for step in range(ITERS):
        log_total = jnp.zeros(estimate.shape, jnp.float32)
        for view_at in range(VIEWS):
            blurred = separable(current, normed[view_at])
            ratio = observed[view_at] / blurred
            correction = separable(ratio, flipped[view_at])
            log_total = log_total + jnp.log(correction)
        current = current * jnp.exp(log_total / VIEWS)
    return current
```

```python
import jax
import jax.numpy as jnp
from jax import lax
from jax.experimental import pallas as pl
from jax.experimental.pallas import tpu as pltpu
from jax.sharding import PartitionSpec as P

ITERS = 2
LANES = 128
BF = jnp.bfloat16
F32 = jnp.float32
VMEM = pl.BlockSpec(memory_space=pltpu.VMEM)
SMEM = pl.BlockSpec(memory_space=pltpu.SMEM)


def shaped(shape, dtype=F32):
    return jax.ShapeDtypeStruct(shape, dtype)


def split(cells):
    high = cells.astype(BF)
    return high, (cells - high.astype(F32)).astype(BF)


def block_at(view, place, blocks):
    at = jnp.where(view == 0, place, blocks - 1 - place)
    return pl.ds(pl.multiple_of(at * LANES, LANES), LANES)


def fold(planes, view, parts):
    piece = LANES // parts
    lane = lax.broadcasted_iota(jnp.int32, planes[0].shape, 1)
    first = jnp.where(view == 0, 0, piece)
    total = None
    for at, plane in enumerate(planes):
        moved = pltpu.roll(plane, lax.rem(first + at * piece, LANES), 1)
        total = moved if total is None else jnp.where(lane >= at * piece, moved, total)
    return total


def unfold(folded, view, parts, at):
    piece = LANES // parts
    first = jnp.where(view == 0, LANES, LANES - piece)
    return pltpu.roll(folded, lax.rem(first - at * piece, LANES), 1)


def pack_window(view, planes_of, depth, own, parts, out_ref):
    for place in range(own):
        for z in range(depth):
            out_ref[place * depth + z] = planes_of(z, place)
    for group in range(depth // parts):
        planes = [planes_of(group * parts + at, own) for at in range(parts)]
        out_ref[own * depth + group] = fold(planes, view, parts)


def unpack_window(view, packed_of, depth, own, parts, store):
    for place in range(own):
        for z in range(depth):
            store(z, place, packed_of(place * depth + z))
    for group in range(depth // parts):
        folded = packed_of(own * depth + group)
        for at in range(parts):
            store(group * parts + at, own, unfold(folded, view, parts, at))


def est_pack_kernel(meta, est, out):
    depth, _, width = est.shape
    own = width // LANES // 2
    view = meta[0]
    pack_window(
        view, lambda z, p: est[z, :, block_at(view, p, width // LANES)], depth, own, 2, out
    )


def obs_pack_kernel(meta, obs, mine, theirs):
    _, depth, _, width = obs.shape
    own = width // LANES // 2
    for view, out in ((meta[0], mine), (1 - meta[0], theirs)):
        pack_window(
            view,
            lambda z, p, view=view: obs[0, z, :, block_at(view, p, width // LANES)],
            depth,
            own,
            2,
            out,
        )


def bands_kernel(meta, taps, y_out, x_out):
    length = taps.shape[1]
    reach = (length - 1) // 2
    rows = y_out.shape[1]
    span = 2 * rows
    x_out[...] = jnp.zeros_like(x_out)
    low = (LANES - reach) // 16 * 16
    high = -(-(2 * LANES + reach) // 16) * 16
    at_before = pl.multiple_of(jnp.where(meta[0] == 0, low, 2 * LANES + low), 16)
    at_after = pl.multiple_of(jnp.where(meta[0] == 0, 2 * LANES, 0), 16)
    in_at = lax.broadcasted_iota(jnp.int32, (high - low, LANES), 0) + low
    out_at = lax.broadcasted_iota(jnp.int32, (high - low, LANES), 1)
    lag = in_at - LANES - out_at
    r_at = lax.broadcasted_iota(jnp.int32, (rows, 3 * span), 0)
    s_at = lax.broadcasted_iota(jnp.int32, (rows, 3 * span), 1)
    y_lag = lax.rem(s_at, span) - r_at - rows // 2
    for back in range(2):
        x_band = jnp.zeros(lag.shape, F32)
        y_band = jnp.zeros(y_lag.shape, F32)
        for tap in range(length):
            at = tap - reach if back == 0 else reach - tap
            x_band = jnp.where(lag == at, taps[2, tap], x_band)
            y_band = jnp.where(y_lag == at, taps[1, tap], y_band)
        x_high, x_low = split(x_band)
        for which, cells in enumerate((x_high, x_low)):
            before, after = LANES - low, high - 2 * LANES
            x_out[back, which, pl.ds(at_before, before)] = cells[:before]
            x_out[back, which, LANES : 2 * LANES] = cells[before : before + LANES]
            x_out[back, which, pl.ds(at_after, after)] = cells[before + LANES :]
        y_high = y_band.astype(BF).astype(F32)
        y_out[back] = jnp.where(s_at < 2 * span, y_high, y_band - y_high).astype(BF)


def spread_x(x_bands, back, own_mat, ext_mat):
    own = own_mat.shape[1] // LANES
    for part, which in enumerate((0, 1, 0)):
        for src in range(own + 1):
            at = (part * (own + 1) + src) * LANES
            for dst in range(own):
                if abs(src - dst) <= 1:
                    start = (src - dst + 1) * LANES
                    cells = x_bands[back, which, start : start + LANES, :]
                else:
                    cells = jnp.zeros((LANES, LANES), BF)
                own_mat[at : at + LANES, dst * LANES : (dst + 1) * LANES] = cells
        if ext_mat is not None:
            for src in range(2):
                at = (part * 2 + src) * LANES
                ext_mat[at : at + LANES, :] = x_bands[back, which, src * LANES : (src + 1) * LANES, :]


def y_stage(source, bands, lanes):
    high, low = split(source)
    return jnp.dot(bands, jnp.concatenate([high, low, high], axis=0), preferred_element_type=F32)


def z_stage(taps, view, back, inner, base, rows, outer):
    depth = inner.shape[0]
    reach = (taps.shape[1] - 1) // 2
    for row in range(0, rows, 8):
        planes = [inner[z, base + row : base + row + 8, :] for z in range(depth)]
        for out in range(depth):
            total = None
            for z in range(depth):
                at = reach + (out - z if back else z - out)
                term = taps[view, at] * planes[z]
                total = term if total is None else total + term
            outer[out, row : row + 8, :] = total


def x_stage(cells, own_mat, ext_mat):
    depth, rows, lanes = cells.shape
    flat = cells.reshape(depth * rows, lanes)
    high, low = split(flat)
    left = jnp.concatenate([high, high, low], axis=1)
    own = jnp.dot(left, own_mat[...], preferred_element_type=F32).reshape(depth, rows, -1)
    if ext_mat is None:
        return own, None
    at = lanes - 2 * LANES
    left = jnp.concatenate([high[:, at:], high[:, at:], low[:, at:]], axis=1)
    ext = jnp.dot(left, ext_mat[...], preferred_element_type=F32).reshape(depth, rows, LANES)
    return own, ext


def forward(field, z_taps, y_bands, x_mats, inner, outer, emit):
    depth = field.shape[0]
    rows = outer.shape[1]
    for half in range(2):
        for z in range(depth):
            inner[z] = y_stage(field[z, half * rows : half * rows + 2 * rows, :], y_bands, None)
        for view in range(2):
            z_stage(z_taps, view, False, inner, view * rows, rows, outer)
            own, ext = x_stage(outer[...], *x_mats[view])
            emit(view, half, own, ext)


def backward(ratio, view, z_taps, y_band, x_mat, inner, outer):
    depth = ratio.shape[0]
    rows = outer.shape[1]
    for z in range(depth):
        inner[z, :rows, :] = y_stage(ratio[z], y_band, None)
    z_stage(z_taps, view, True, inner, 0, rows, outer)
    return x_stage(outer[...], *x_mat)


def place_rows(even, rows):
    at_a = pl.multiple_of(jnp.where(even == 1, 2 * rows, 0), rows)
    at_b = pl.multiple_of(jnp.where(even == 1, 0, 2 * rows), rows)
    return at_a, at_b


def forward_kernel(meta, z_taps, est, got_a, got_b, y0, y1, x0, x1, blurred, field, inner, outer, *mats):
    depth, rows, width = est.shape
    own = width // LANES // 2
    view = meta[0]
    for place in range(own + 1):
        lanes = slice(place * LANES, (place + 1) * LANES)
        field[:, rows : 2 * rows, lanes] = est[:, :, block_at(view, place, width // LANES)]
    for got, at in zip((got_a, got_b), place_rows(meta[1], rows)):

        def store(z, place, cells, at=at):
            field[z, pl.ds(at, rows), place * LANES : (place + 1) * LANES] = cells

        unpack_window(view, lambda n, got=got: got[n], depth, own, 2, store)
    spread_x(x0, 0, mats[0], mats[1])
    spread_x(x1, 0, mats[2], mats[3])
    y_bands = jnp.concatenate([y0[0], y1[0]], axis=0)

    def emit(v, half, own_cells, ext):
        blurred[v, :, half * rows : (half + 1) * rows, : own * LANES] = own_cells
        blurred[v, :, half * rows : (half + 1) * rows, own * LANES :] = ext

    forward(field, z_taps, y_bands, ((mats[0], mats[1]), (mats[2], mats[3])), inner, outer, emit)


def fill_observed(meta, obs_own, obs_other, halo_a, halo_b, obs, rows, own, depth):
    view = meta[0]
    near = rows // 2
    count = obs_own.shape[0]
    at_a = pl.multiple_of(jnp.where(meta[1] == 1, rows + near, 0), near)
    at_b = pl.multiple_of(jnp.where(meta[1] == 1, 0, rows + near), near)
    for which, middle in enumerate((obs_own, obs_other)):
        slot = jnp.where(view == 0, which, 1 - which)

        def store(z, place, cells):
            obs[slot, z, near : near + rows, place * LANES : (place + 1) * LANES] = cells

        unpack_window(view, lambda n: middle[n], depth, own, 2, store)
        for halo, at in ((halo_a, at_a), (halo_b, at_b)):

            def store_halo(z, place, cells):
                obs[slot, z, pl.ds(at, near), place * LANES : (place + 1) * LANES] = cells

            unpack_window(view, lambda n: halo[which * count + n], depth, own, 2, store_halo)


def row_mask(meta, rows, lanes):
    at = lax.broadcasted_iota(jnp.int32, (2 * rows, lanes), 0)
    low = jnp.where(meta[2] == 1, rows // 2, 0)
    high = jnp.where(meta[3] == 1, rows + rows // 2, 2 * rows)
    return (at >= low) & (at < high)


def first_back_kernel(
    meta, z_taps, est, blurred, obs_own, obs_other, halo_a, halo_b, y0, y1, x0, x1,
    obs, current, to_send, ratio, inner, outer, *mats
):
    depth, rows, width = est.shape
    own = width // LANES // 2
    lanes = (own + 1) * LANES
    view = meta[0]
    fill_observed(meta, obs_own, obs_other, halo_a, halo_b, obs, rows, own, depth)
    spread_x(x0, 1, mats[0], mats[1])
    spread_x(x1, 1, mats[2], mats[3])
    inside = row_mask(meta, rows, lanes)
    gains = []
    for v in range(2):
        for z in range(depth):
            ratio[z] = jnp.where(inside, obs[v, z] / blurred[v, z], 0.0)
        y_band = (y0, y1)[v][1]
        gains.append(backward(ratio, v, z_taps, y_band, mats[2 * v : 2 * v + 2], inner, outer))
    root_own = jnp.sqrt(gains[0][0] * gains[1][0])
    root_ext = jnp.sqrt(gains[0][1] * gains[1][1])
    for place in range(own + 1):
        cells = est[:, :, block_at(view, place, width // LANES)]
        factor = root_ext if place == own else root_own[:, :, place * LANES : (place + 1) * LANES]
        current[:, :, place * LANES : (place + 1) * LANES] = cells * factor
    pack_window(
        view, lambda z, p: current[z, :, p * LANES : (p + 1) * LANES], depth, own, 4, to_send
    )


def second_kernel(
    meta, z_taps, current, got_a, got_b, obs, y0, y1, x0, x1,
    out, field, ratios, inner, outer, *mats
):
    depth, rows, lanes = current.shape
    own = lanes // LANES - 1
    view = meta[0]
    field[:, rows : 2 * rows, :] = current[...]
    for got, at in zip((got_a, got_b), place_rows(meta[1], rows)):

        def store(z, place, cells, at=at):
            field[z, pl.ds(at, rows), place * LANES : (place + 1) * LANES] = cells

        unpack_window(view, lambda n, got=got: got[n], depth, own, 4, store)
    spread_x(x0, 0, mats[0], mats[1])
    spread_x(x1, 0, mats[2], mats[3])
    spread_x(x0, 1, mats[4], None)
    spread_x(x1, 1, mats[5], None)
    y_bands = jnp.concatenate([y0[0], y1[0]], axis=0)
    inside = row_mask(meta, rows, LANES)

    def emit(v, half, own_cells, ext):
        at = slice(half * rows, (half + 1) * rows)
        mask = inside[at]
        for place in range(own + 1):
            cols = slice(place * LANES, (place + 1) * LANES)
            cells = ext if place == own else own_cells[:, :, cols]
            ratios[v, :, at, cols] = jnp.where(mask[None], obs[v, :, at, cols] / cells, 0.0)

    forward(field, z_taps, y_bands, ((mats[0], mats[1]), (mats[2], mats[3])), inner, outer, emit)
    gains = []
    for v in range(2):
        y_band = (y0, y1)[v][1]
        gains.append(
            backward(ratios.at[v], v, z_taps, y_band, (mats[4 + v], None), inner, outer)[0]
        )
    result = current[:, :, : own * LANES] * jnp.sqrt(gains[0] * gains[1])
    for place in range(own):
        at = jnp.where(view == 0, place, own - 1 - place)
        out[:, :, pl.ds(pl.multiple_of(at * LANES, LANES), LANES)] = result[
            :, :, place * LANES : (place + 1) * LANES
        ]


def paired(cells_a, cells_b):
    count = lax.axis_size("tile")
    pairs_a = [(i, i ^ 1) for i in range(count)]
    pairs_b = []
    for i in range(1, count - 1, 2):
        pairs_b += [(i, i + 1), (i + 1, i)]
    got_b = lax.ppermute(cells_b, "tile", pairs_b)
    got_a = lax.ppermute(cells_a, "tile", pairs_a)
    return got_a, got_b


def two_view_body(estimate, observed, psf_taps):
    depth, rows, width = estimate.shape
    blocks = width // LANES
    own = blocks // 2
    lanes = (own + 1) * LANES
    length = psf_taps.shape[2]
    view = lax.axis_index("view")
    tile = lax.axis_index("tile")
    last = lax.axis_size("tile") - 1
    even = 1 - lax.rem(tile, 2)
    swap = [(0, 1), (1, 0)]
    meta = jnp.stack([view, even, tile == 0, tile == last]).astype(jnp.int32)
    count = own * depth + depth // 2
    count_mid = own * depth + depth // 4

    other_taps = lax.ppermute(psf_taps, "view", swap)
    est_send = pl.pallas_call(
        est_pack_kernel, out_shape=shaped((count, rows, LANES)), in_specs=[SMEM, VMEM],
        out_specs=VMEM, name="est_pack",
    )(meta, estimate)
    est_a, est_b = paired(est_send, est_send)
    mine, theirs = pl.pallas_call(
        obs_pack_kernel, out_shape=[shaped((count, rows, LANES))] * 2, in_specs=[SMEM, VMEM],
        out_specs=[VMEM, VMEM], name="obs_pack",
    )(meta, observed)
    other = lax.ppermute(theirs, "view", swap)
    both = jnp.concatenate([mine, other], axis=0)
    near = rows // 2
    halo_a, halo_b = paired(
        lax.dynamic_slice_in_dim(both, even * near, near, 1),
        lax.dynamic_slice_in_dim(both, (1 - even) * near, near, 1),
    )

    taps = jnp.where(
        view == 0,
        jnp.concatenate([psf_taps, other_taps], axis=0),
        jnp.concatenate([other_taps, psf_taps], axis=0),
    )
    normed = taps / jnp.sum(taps, axis=2, keepdims=True)
    z_taps = normed[:, 0]
    bands = [
        pl.pallas_call(
            bands_kernel,
            out_shape=[shaped((2, rows, 6 * rows), BF), shaped((2, 2, 3 * LANES, LANES), BF)],
            in_specs=[SMEM, SMEM], out_specs=[VMEM, VMEM], name="bands",
        )(meta, normed[v])
        for v in range(2)
    ]
    mats = [bands[0][0], bands[1][0], bands[0][1], bands[1][1]]
    own_mat = pltpu.VMEM((3 * lanes, own * LANES), BF)
    ext_mat = pltpu.VMEM((6 * LANES, LANES), BF)
    inner = pltpu.VMEM((depth, 2 * rows, lanes), F32)
    outer = pltpu.VMEM((depth, rows, lanes), F32)

    blurred = pl.pallas_call(
        forward_kernel, out_shape=shaped((2, depth, 2 * rows, lanes)),
        in_specs=[SMEM, SMEM] + [VMEM] * 7, out_specs=VMEM,
        scratch_shapes=[pltpu.VMEM((depth, 3 * rows, lanes), F32), inner, outer] + [own_mat, ext_mat] * 2,
        name="first_forward",
    )(meta, z_taps, estimate, est_a, est_b, *mats)
    obs, current, cur_send = pl.pallas_call(
        first_back_kernel,
        out_shape=[
            shaped((2, depth, 2 * rows, lanes)), shaped((depth, rows, lanes)), shaped((count_mid, rows, LANES)),
        ],
        in_specs=[SMEM, SMEM] + [VMEM] * 10, out_specs=[VMEM] * 3,
        scratch_shapes=[pltpu.VMEM((depth, 2 * rows, lanes), F32), inner, outer] + [own_mat, ext_mat] * 2,
        name="first_back",
    )(meta, z_taps, estimate, blurred, mine, other, halo_a, halo_b, *mats)
    cur_a, cur_b = paired(cur_send, cur_send)
    half = pl.pallas_call(
        second_kernel, out_shape=shaped((depth, rows, own * LANES)),
        in_specs=[SMEM, SMEM] + [VMEM] * 8, out_specs=VMEM,
        scratch_shapes=[
            pltpu.VMEM((depth, 3 * rows, lanes), F32), pltpu.VMEM((2, depth, 2 * rows, lanes), F32),
            inner, outer,
        ] + [own_mat, ext_mat] * 2 + [own_mat] * 2,
        name="second",
    )(meta, z_taps, current, cur_a, cur_b, obs, *mats)
    far = lax.ppermute(half, "view", swap)
    return jnp.where(
        view == 0, jnp.concatenate([half, far], axis=2), jnp.concatenate([far, half], axis=2)
    )


def extended_2(cells, sides, width):
    for axis, dim in sides:
        count = lax.axis_size(axis)
        ends = count - 1
        head = lax.slice_in_dim(cells, 0, width, axis=dim)
        tail = lax.slice_in_dim(cells, cells.shape[dim] - width, cells.shape[dim], axis=dim)
        cells = jnp.concatenate(
            [
                lax.ppermute(tail, axis, [(i, (i + 1) % count) for i in range(ends)]),
                cells,
                lax.ppermute(head, axis, [((i + 1) % count, i) for i in range(ends)]),
            ],
            axis=dim,
        )
    return cells


def band_matrix(taps, count_in, count_out, offset):
    rows_in = jnp.arange(count_in)[:, None]
    cols_out = jnp.arange(count_out)[None, :]
    lag = rows_in - cols_out + offset
    length = taps.shape[0]
    inside = (lag >= 0) & (lag < length)
    return jnp.where(inside, jnp.take(taps, jnp.clip(lag, 0, length - 1)), 0.0)


def many_bands(taps, count_in, count_out, offset):
    return jax.vmap(lambda one: band_matrix(one, count_in, count_out, offset))(taps)


def blur(field, z_mats, y_mats, x_taps, cols_out):
    highest = lax.Precision.HIGHEST
    if field.ndim == 3:
        out = jnp.einsum("kyx,vkz->vzyx", field, z_mats, precision=highest)
    else:
        out = jnp.einsum("vkyx,vkz->vzyx", field, z_mats, precision=highest)
    out = jnp.einsum("vzjx,vjy->vzyx", out, y_mats, precision=highest)
    reach = (x_taps.shape[1] - 1) // 2
    pieces = []
    for start in range(0, cols_out, 128):
        block = min(128, cols_out - start)
        x_mats = many_bands(x_taps, block + 2 * reach, block, 0)
        piece = lax.slice_in_dim(out, start, start + block + 2 * reach, axis=3)
        pieces.append(jnp.einsum("vzyj,vjx->vzyx", piece, x_mats, precision=highest))
    return jnp.concatenate(pieces, axis=3)


def body(estimate, observed, psf_taps):
    depth, rows, width = estimate.shape
    half = (psf_taps.shape[2] - 1) // 2
    views = lax.axis_size("view")
    recorded = lax.all_to_all(observed, "view", split_axis=3, concat_axis=0, tiled=True)
    taps = lax.all_gather(psf_taps, "view", axis=0, tiled=True)
    cols = width // views
    col_start = lax.axis_index("view") * cols
    current = lax.dynamic_slice_in_dim(estimate, col_start, cols, 2)
    normed = taps / jnp.sum(taps, axis=2, keepdims=True)
    flipped = normed[:, :, ::-1]
    fwd_z = many_bands(normed[:, 0], depth, depth, half)
    back_z = many_bands(flipped[:, 0], depth, depth, half)
    back_y = many_bands(flipped[:, 1], rows + 2 * half, rows, 0)
    fwd_y = many_bands(normed[:, 1], rows + 2 * half, rows, 0)
    for step in range(ITERS):
        extended = extended_2(current, (("view", 2), ("tile", 1)), half)
        blurred = blur(extended, fwd_z, fwd_y, normed[:, 2], cols)
        ratio = recorded / blurred
        ratio_ext = extended_2(ratio, (("view", 3), ("tile", 2)), half)
        log_corr = jnp.log(blur(ratio_ext, back_z, back_y, flipped[:, 2], cols))
        log_total = jnp.sum(log_corr, axis=0)
        current = current * jnp.exp(log_total / views)
    current = lax.all_gather(current, "view", axis=2, tiled=True)
    return current


def fits(mesh, estimate, psf_taps):
    depth, rows, width = estimate.shape
    tiles = mesh.shape["tile"]
    reach = (psf_taps.shape[2] - 1) // 2
    return (
        mesh.shape["view"] == 2
        and tiles % 2 == 0
        and rows % (32 * tiles) == 0
        and rows // tiles >= 2 * (reach + 1)
        and width % (2 * LANES) == 0
        and 4 * reach <= LANES // 2
        and 2 * reach <= LANES // 4
        and depth % 4 == 0
    )


def solution(mesh):
    placed = (P(None, "tile", None), P("view", None, "tile", None), P("view", None, None))

    def run(estimate, observed, psf_taps):
        chosen = two_view_body if fits(mesh, estimate, psf_taps) else body
        return jax.shard_map(
            chosen, mesh=mesh, in_specs=placed, out_specs=P(None, "tile", None), check_vma=False
        )(estimate, observed, psf_taps)

    return run
```

```python
import jax
import jax.numpy as jnp
from jax import lax
from jax.experimental import pallas as pl
from jax.experimental.pallas import tpu as pltpu
from jax.sharding import PartitionSpec as P


ITERS = 2
LANES = 128
VMEM_BYTES = 24 << 20
BF = jnp.bfloat16
F32 = jnp.float32
VMEM = pl.BlockSpec(memory_space=pltpu.VMEM)
SMEM = pl.BlockSpec(memory_space=pltpu.SMEM)
HBM = pl.BlockSpec(memory_space=pltpu.HBM)


def shaped(shape, dtype=F32):
    return jax.ShapeDtypeStruct(shape, dtype)


def call(kernel, outs, in_specs, out_specs=None, scratch=(), **more):
    return pl.pallas_call(
        kernel, out_shape=outs, in_specs=in_specs,
        out_specs=out_specs or jax.tree.map(lambda _: VMEM, outs), scratch_shapes=scratch,
        compiler_params=pltpu.CompilerParams(vmem_limit_bytes=VMEM_BYTES), **more,
    )


def in_hbm(cells):
    return pltpu.with_memory_space_constraint(cells, pltpu.HBM)


def split(cells):
    high = cells.astype(BF)
    return high, (cells - high.astype(F32)).astype(BF)


def block_at(view, place, blocks):
    at = jnp.where(view == 0, place, blocks - 1 - place)
    return pl.ds(pl.multiple_of(at * LANES, LANES), LANES)


def fold(planes, view, parts):
    piece = LANES // parts
    lane = lax.broadcasted_iota(jnp.int32, planes[0].shape, 1)
    first = jnp.where(view == 0, 0, piece)
    total = None
    for at, plane in enumerate(planes):
        moved = pltpu.roll(plane, lax.rem(first + at * piece, LANES), 1)
        total = moved if total is None else jnp.where(lane >= at * piece, moved, total)
    return total


def unfold(folded, view, parts, at):
    piece = LANES // parts
    first = jnp.where(view == 0, LANES, LANES - piece)
    return pltpu.roll(folded, lax.rem(first - at * piece, LANES), 1)


def pack_window(view, planes_of, depth, own, parts, out_ref):
    for place in range(own):
        for z in range(depth):
            out_ref[place * depth + z] = planes_of(z, place)
    for group in range(depth // parts):
        planes = [planes_of(group * parts + at, own) for at in range(parts)]
        out_ref[own * depth + group] = fold(planes, view, parts)


def unpack_window(view, packed_of, depth, own, parts, store):
    for place in range(own):
        for z in range(depth):
            store(z, place, packed_of(place * depth + z))
    for group in range(depth // parts):
        folded = packed_of(own * depth + group)
        for at in range(parts):
            store(group * parts + at, own, unfold(folded, view, parts, at))


def load_kernel(meta, obs_hbm, est_hbm, taps, obs, est, theirs, obs_sems, est_sem):
    _, depth, _, width = obs.shape
    own = width // LANES // 2
    view = 1 - meta[0]
    copies = [
        pltpu.make_async_copy(obs_hbm.at[:, pl.ds(z, 1)], obs.at[:, pl.ds(z, 1)], obs_sems.at[z])
        for z in range(depth)
    ]
    for copy in copies:
        copy.start()
    est_copy = pltpu.make_async_copy(est_hbm, est, est_sem)
    est_copy.start()
    _, kinds, length = taps.shape
    theirs[own * depth + depth // 2] = jnp.zeros_like(theirs[0])
    theirs[own * depth + depth // 2, :kinds, :length] = taps[0]
    for z in range(0, depth, 2):
        copies[z].wait()
        copies[z + 1].wait()
        for at in (z, z + 1):
            for place in range(own):
                theirs[place * depth + at] = obs[0, at, :, block_at(view, place, width // LANES)]
        ends = [obs[0, at, :, block_at(view, own, width // LANES)] for at in (z, z + 1)]
        theirs[own * depth + z // 2] = fold(ends, view, 2)
    est_copy.wait()


def near_rows(even, rows):
    near = rows // 2
    at_a = pl.multiple_of(jnp.where(even == 1, near, 0), near)
    at_b = pl.multiple_of(jnp.where(even == 1, 0, near), near)
    return at_a, at_b


def pack_kernel(meta, est, send):
    depth, _, width = est.shape
    blocks = width // LANES
    pack_window(
        meta[0], lambda z, p: est[z, :, block_at(meta[0], p, blocks)], depth, blocks // 2, 2, send
    )


def pack_near_kernel(meta, obs, send_a, send_b):
    _, depth, rows, width = obs.shape
    blocks = width // LANES
    near = rows // 2
    for send, at in zip((send_a, send_b), near_rows(meta[1], rows)):
        pack_window(
            meta[0],
            lambda z, p, at=at: obs[0, z, pl.ds(at, near), block_at(meta[0], p, blocks)],
            depth, blocks // 2, 2, send,
        )


def bands_kernel(meta, taps, y_out, own_mats, ext_mats, band):
    length = taps.shape[2]
    reach = (length - 1) // 2
    rows = y_out.shape[2]
    span = 2 * rows
    low = (LANES - reach) // 16 * 16
    high = -(-(2 * LANES + reach) // 16) * 16
    before, after = LANES - low, high - 2 * LANES
    at_before = pl.multiple_of(jnp.where(meta[0] == 0, low, 2 * LANES + low), 16)
    at_after = pl.multiple_of(jnp.where(meta[0] == 0, 2 * LANES, 0), 16)
    lag = (
        lax.broadcasted_iota(jnp.int32, (high - low, LANES), 0)
        + (low - LANES)
        - lax.broadcasted_iota(jnp.int32, (high - low, LANES), 1)
    )
    r_at = lax.broadcasted_iota(jnp.int32, (rows, 3 * span), 0)
    s_at = lax.broadcasted_iota(jnp.int32, (rows, 3 * span), 1)
    y_lag = lax.rem(s_at, span) - r_at - rows // 2
    band[...] = jnp.zeros_like(band)
    for view in range(2):
        for back in range(2):
            x_band = jnp.zeros(lag.shape, F32)
            y_band = jnp.zeros(y_lag.shape, F32)
            for tap in range(length):
                at = tap - reach if back == 0 else reach - tap
                x_band = jnp.where(lag == at, taps[view, 2, tap], x_band)
                y_band = jnp.where(y_lag == at, taps[view, 1, tap], y_band)
            for which, cells in enumerate(split(x_band)):
                band[which, pl.ds(at_before, before)] = cells[:before]
                band[which, LANES : 2 * LANES] = cells[before : before + LANES]
                band[which, pl.ds(at_after, after)] = cells[before + LANES :]
            spread_x(band, own_mats.at[view, back], ext_mats.at[view, back])
            y_high = y_band.astype(BF).astype(F32)
            y_out[view, back] = jnp.where(s_at < 2 * span, y_high, y_band - y_high).astype(BF)


def spread_x(band, own_mat, ext_mat):
    own = own_mat.shape[1] // LANES
    for part, which in enumerate((0, 1, 0)):
        for src in range(own + 1):
            at = (part * (own + 1) + src) * LANES
            for dst in range(own):
                if abs(src - dst) <= 1:
                    start = (src - dst + 1) * LANES
                    cells = band[which, start : start + LANES, :]
                else:
                    cells = jnp.zeros((LANES, LANES), BF)
                own_mat[at : at + LANES, dst * LANES : (dst + 1) * LANES] = cells
        for src in range(2):
            at = (part * 2 + src) * LANES
            ext_mat[at : at + LANES, :] = band[which, src * LANES : (src + 1) * LANES, :]


def y_stage(source, bands):
    high, low = split(source)
    return jnp.dot(bands, jnp.concatenate([high, low, high], axis=0), preferred_element_type=F32)


def z_stage(taps, view, back, inner, base, rows, outer):
    depth = inner.shape[0]
    reach = (taps.shape[1] - 1) // 2
    for row in range(0, rows, 8):
        planes = [inner[z, base + row : base + row + 8, :] for z in range(depth)]
        for out in range(depth):
            total = None
            for z in range(depth):
                at = reach + (out - z if back else z - out)
                term = taps[view, at] * planes[z]
                total = term if total is None else total + term
            outer[out, row : row + 8, :] = total


def x_stage(cells, own_mat, ext_mat):
    depth, rows, lanes = cells.shape
    flat = cells.reshape(depth * rows, lanes)
    high, low = split(flat)
    left = jnp.concatenate([high, high, low], axis=1)
    own = jnp.dot(left, own_mat[...], preferred_element_type=F32).reshape(depth, rows, -1)
    if ext_mat is None:
        return own, None
    at = lanes - 2 * LANES
    left = jnp.concatenate([high[:, at:], high[:, at:], low[:, at:]], axis=1)
    ext = jnp.dot(left, ext_mat[...], preferred_element_type=F32).reshape(depth, rows, LANES)
    return own, ext


def forward(field, z_taps, y_bands, own_mats, ext_mats, inner, outer, emit):
    depth = field.shape[0]
    rows = outer.shape[2]
    both = jnp.concatenate([y_bands[0, 0], y_bands[1, 0]], axis=0)
    for half in range(2):
        for z in range(depth):
            inner[half, z] = y_stage(field[z, half * rows : half * rows + 2 * rows, :], both)
        for view in range(2):
            z_stage(z_taps, view, False, inner.at[half], view * rows, rows, outer.at[view])
            emit(view, half, *x_stage(outer[view], own_mats.at[view, 0], ext_mats.at[view, 0]))


def backward(ratio, view, z_taps, y_bands, own_mats, ext_mats, inner, outer):
    depth = ratio.shape[0]
    rows = outer.shape[2]
    for z in range(depth):
        inner[view, z, :rows, :] = y_stage(ratio[z], y_bands[view, 1])
    z_stage(z_taps, view, True, inner.at[view], 0, rows, outer.at[view])
    ext_mat = None if ext_mats is None else ext_mats.at[view, 1]
    return x_stage(outer[view], own_mats.at[view, 1], ext_mat)


def block_rows(even, rows):
    at_a = pl.multiple_of(jnp.where(even == 1, 2 * rows, 0), rows)
    at_b = pl.multiple_of(jnp.where(even == 1, 0, 2 * rows), rows)
    return at_a, at_b


def halo_rows(even, rows):
    near = rows // 2
    at_a = pl.multiple_of(jnp.where(even == 1, rows + near, 0), near)
    at_b = pl.multiple_of(jnp.where(even == 1, 0, rows + near), near)
    return at_a, at_b


def cols(place):
    return slice(place * LANES, (place + 1) * LANES)


def row_mask(meta, rows, lanes):
    at = lax.broadcasted_iota(jnp.int32, (2 * rows, lanes), 0)
    low = jnp.where(meta[2] == 1, rows // 2, 0)
    high = jnp.where(meta[3] == 1, rows + rows // 2, 2 * rows)
    return (at >= low) & (at < high)


def first_kernel(
    meta, z_taps, est, obs_own, got_a, got_b, own_a, own_b, other, y_bands, own_mats, ext_mats,
    obs, ratio, gain, field, inner, outer
):
    depth, rows, width = est.shape
    own = width // LANES // 2
    view = meta[0]
    near = rows // 2
    mid = slice(near, near + rows)
    for place in range(own + 1):
        from_lanes = block_at(view, place, width // LANES)
        field[:, rows : 2 * rows, cols(place)] = est[:, :, from_lanes]
        obs[0, :, mid, cols(place)] = obs_own[0, :, :, from_lanes]

    def store_other(z, place, cells):
        obs[1, z, mid, cols(place)] = cells

    unpack_window(view, lambda n: other[n], depth, own, 2, store_other)
    ends = zip(
        (got_a, got_b), (own_a, own_b), block_rows(meta[1], rows), halo_rows(meta[1], rows)
    )
    for got, got_halo, at, at_halo in ends:

        def store(z, place, cells, at=at):
            field[z, pl.ds(at, rows), cols(place)] = cells

        def store_halo(z, place, cells, at=at_halo):
            obs[0, z, pl.ds(at, near), cols(place)] = cells

        unpack_window(view, lambda n, got=got: got[n], depth, own, 2, store)
        unpack_window(view, lambda n, got=got_halo: got[n], depth, own, 2, store_halo)
    inside = row_mask(meta, rows, LANES)

    def emit(v, half, own_cells, ext):
        at = slice(half * rows, (half + 1) * rows)
        for place in range(own + 1):
            cells = ext if place == own else own_cells[:, :, cols(place)]
            if v == 0:
                mask = inside[at]
                ratio[0, :, at, cols(place)] = jnp.where(
                    mask[None], obs[0, :, at, cols(place)] / cells, 0.0
                )
            else:
                halo = slice(0, near) if half == 0 else slice(near, rows)
                keep = slice(near, rows) if half == 0 else slice(0, near)
                base = half * rows
                halo_at = slice(base + halo.start, base + halo.stop)
                keep_at = slice(base + keep.start, base + keep.stop)
                ratio[1, :, halo_at, cols(place)] = cells[:, halo]
                ratio[1, :, keep_at, cols(place)] = obs[1, :, keep_at, cols(place)] / cells[:, keep]

    forward(field, z_taps, y_bands, own_mats, ext_mats, inner, outer, emit)
    back = backward(ratio.at[0], 0, z_taps, y_bands, own_mats, ext_mats, inner, outer)
    gain[:, :, : own * LANES] = back[0]
    gain[:, :, own * LANES :] = back[1]


def update_kernel(
    meta, z_taps, est, gain, obs_in, ratio_in, halo_a, halo_b, y_bands, own_mats, ext_mats,
    obs, ratio, current, to_send, inner, outer
):
    depth, rows, width = est.shape
    own = width // LANES // 2
    view = meta[0]
    near = rows // 2
    for halo, at in zip((halo_a, halo_b), halo_rows(meta[1], rows)):
        known = jnp.where(at == 0, 1 - meta[2], 1 - meta[3]) == 1

        def store(z, place, cells, at=at, known=known):
            obs[1, z, pl.ds(at, near), cols(place)] = cells
            blurred = ratio_in[1, z, pl.ds(at, near), cols(place)]
            ratio[1, z, pl.ds(at, near), cols(place)] = jnp.where(known, cells / blurred, 0.0)

        unpack_window(view, lambda n, halo=halo: halo[n], depth, own, 2, store)
    back = backward(ratio.at[1], 1, z_taps, y_bands, own_mats, ext_mats, inner, outer)
    for place in range(own + 1):
        cells = est[:, :, block_at(view, place, width // LANES)]
        other = back[1] if place == own else back[0][:, :, cols(place)]
        current[:, :, cols(place)] = cells * jnp.sqrt(gain[:, :, cols(place)] * other)
    pack_window(view, lambda z, p: current[z, :, cols(p)], depth, own, 4, to_send)


def second_kernel(
    meta, z_taps, current, got_a, got_b, obs, y_bands, own_mats, ext_mats,
    out, field, ratios, inner, outer
):
    depth, rows, lanes = current.shape
    own = lanes // LANES - 1
    view = meta[0]
    field[:, rows : 2 * rows, :] = current[...]
    for got, at in zip((got_a, got_b), block_rows(meta[1], rows)):

        def store(z, place, cells, at=at):
            field[z, pl.ds(at, rows), cols(place)] = cells

        unpack_window(view, lambda n, got=got: got[n], depth, own, 4, store)
    inside = row_mask(meta, rows, LANES)

    def emit(v, half, own_cells, ext):
        at = slice(half * rows, (half + 1) * rows)
        mask = inside[at]
        for place in range(own + 1):
            cells = ext if place == own else own_cells[:, :, cols(place)]
            ratios[v, :, at, cols(place)] = jnp.where(
                mask[None], obs[v, :, at, cols(place)] / cells, 0.0
            )

    forward(field, z_taps, y_bands, own_mats, ext_mats, inner, outer, emit)
    gains = [
        backward(ratios.at[v], v, z_taps, y_bands, own_mats, None, inner, outer)[0]
        for v in range(2)
    ]
    result = current[:, :, : own * LANES] * jnp.sqrt(gains[0] * gains[1])
    for place in range(own):
        at = jnp.where(view == 0, place, own - 1 - place)
        out[:, :, pl.ds(pl.multiple_of(at * LANES, LANES), LANES)] = result[:, :, cols(place)]


def copy_planes(cells, out, at, sems):
    width = cells.shape[2]
    copies = [
        pltpu.make_async_copy(cells.at[z], out.at[z, :, pl.ds(at, width)], sems.at[z])
        for z in range(cells.shape[0])
    ]
    for copy in copies:
        copy.start()
    for copy in copies:
        copy.wait()


def place_kernel(meta, half, out, sems):
    width = half.shape[2]
    copy_planes(half, out, pl.multiple_of(meta[0] * width, width), sems)


def paired(cells_a, cells_b):
    count = lax.axis_size("tile")
    pairs_a = [(i, i ^ 1) for i in range(count)]
    pairs_b = []
    for i in range(1, count - 1, 2):
        pairs_b += [(i, i + 1), (i + 1, i)]
    got_b = lax.ppermute(cells_b, "tile", pairs_b)
    got_a = lax.ppermute(cells_a, "tile", pairs_a)
    return got_a, got_b


def two_view_body(estimate, observed, psf_taps):
    depth, rows, width = estimate.shape
    own = width // LANES // 2
    lanes = (own + 1) * LANES
    near = rows // 2
    view = lax.axis_index("view")
    tile = lax.axis_index("tile")
    last = lax.axis_size("tile") - 1
    even = 1 - lax.rem(tile, 2)
    swap = [(0, 1), (1, 0)]
    meta = jnp.stack([view, even, tile == 0, tile == last]).astype(jnp.int32)
    count = own * depth + depth // 2
    count_mid = own * depth + depth // 4
    window = shaped((2, depth, 2 * rows, lanes))

    obs_own, est, theirs = call(
        load_kernel,
        [shaped(observed.shape), shaped(estimate.shape), shaped((count + 1, rows, LANES))],
        [SMEM, HBM, HBM, VMEM],
        scratch=[pltpu.SemaphoreType.DMA((depth,)), pltpu.SemaphoreType.DMA],
    )(meta, in_hbm(observed), in_hbm(estimate), psf_taps)
    other = lax.ppermute(theirs, "view", swap)
    other_taps = other[count : count + 1, : psf_taps.shape[1], : psf_taps.shape[2]]
    send = call(pack_kernel, shaped((count, rows, LANES)), [SMEM, VMEM])(meta, est)
    got_a, got_b = paired(send, send)
    own_a, own_b = paired(
        *call(pack_near_kernel, [shaped((count, near, LANES))] * 2, [SMEM, VMEM])(meta, obs_own),
    )

    taps = jnp.concatenate([psf_taps, other_taps], axis=0)
    normed = taps / jnp.sum(taps, axis=2, keepdims=True)
    z_taps = normed[:, 0]
    mats = call(
        bands_kernel,
        [
            shaped((2, 2, rows, 6 * rows), BF),
            shaped((2, 2, 3 * lanes, own * LANES), BF),
            shaped((2, 2, 6 * LANES, LANES), BF),
        ],
        [SMEM, SMEM], scratch=[pltpu.VMEM((2, 3 * LANES, LANES), BF)],
    )(meta, normed)
    halo_a, halo_b = paired(
        lax.dynamic_slice(other, (0, even * near, 0), (count, near, LANES)),
        lax.dynamic_slice(other, (0, (1 - even) * near, 0), (count, near, LANES)),
    )

    stages = [
        pltpu.VMEM((2, depth, 2 * rows, lanes), F32), pltpu.VMEM((2, depth, rows, lanes), F32),
    ]
    field = pltpu.VMEM((depth, 3 * rows, lanes), F32)
    obs, ratio, gain = call(
        first_kernel, [window, window, shaped((depth, rows, lanes))],
        [SMEM, SMEM] + [VMEM] * 10, scratch=[field] + stages,
    )(meta, z_taps, est, obs_own, got_a, got_b, own_a, own_b, other, *mats)
    obs, _, current, cur_send = call(
        update_kernel,
        [window, window, shaped((depth, rows, lanes)), shaped((count_mid, rows, LANES))],
        [SMEM, SMEM] + [VMEM] * 9, scratch=stages, input_output_aliases={4: 0, 5: 1},
    )(meta, z_taps, est, gain, obs, ratio, halo_a, halo_b, *mats)
    cur_a, cur_b = paired(cur_send, cur_send)
    half = call(
        second_kernel, shaped((depth, rows, own * LANES)),
        [SMEM, SMEM] + [VMEM] * 7,
        scratch=[field, pltpu.VMEM((2, depth, 2 * rows, lanes), F32)] + stages,
    )(meta, z_taps, current, cur_a, cur_b, obs, *mats)
    far = lax.ppermute(half, "view", swap)
    partial = call(
        place_kernel, shaped(estimate.shape), [SMEM, VMEM], HBM,
        scratch=[pltpu.SemaphoreType.DMA((depth,))],
    )(meta, half)
    return lax.dynamic_update_slice(partial, far, (0, 0, (1 - view) * own * LANES))


def extended_2(cells, sides, width):
    for axis, dim in sides:
        count = lax.axis_size(axis)
        ends = count - 1
        head = lax.slice_in_dim(cells, 0, width, axis=dim)
        tail = lax.slice_in_dim(cells, cells.shape[dim] - width, cells.shape[dim], axis=dim)
        cells = jnp.concatenate(
            [
                lax.ppermute(tail, axis, [(i, (i + 1) % count) for i in range(ends)]),
                cells,
                lax.ppermute(head, axis, [((i + 1) % count, i) for i in range(ends)]),
            ],
            axis=dim,
        )
    return cells


def band_matrix(taps, count_in, count_out, offset):
    rows_in = jnp.arange(count_in)[:, None]
    cols_out = jnp.arange(count_out)[None, :]
    lag = rows_in - cols_out + offset
    length = taps.shape[0]
    inside = (lag >= 0) & (lag < length)
    return jnp.where(inside, jnp.take(taps, jnp.clip(lag, 0, length - 1)), 0.0)


def many_bands(taps, count_in, count_out, offset):
    return jax.vmap(lambda one: band_matrix(one, count_in, count_out, offset))(taps)


def blur(field, z_mats, y_mats, x_taps, cols_out):
    highest = lax.Precision.HIGHEST
    if field.ndim == 3:
        out = jnp.einsum("kyx,vkz->vzyx", field, z_mats, precision=highest)
    else:
        out = jnp.einsum("vkyx,vkz->vzyx", field, z_mats, precision=highest)
    out = jnp.einsum("vzjx,vjy->vzyx", out, y_mats, precision=highest)
    reach = (x_taps.shape[1] - 1) // 2
    pieces = []
    for start in range(0, cols_out, 128):
        block = min(128, cols_out - start)
        x_mats = many_bands(x_taps, block + 2 * reach, block, 0)
        piece = lax.slice_in_dim(out, start, start + block + 2 * reach, axis=3)
        pieces.append(jnp.einsum("vzyj,vjx->vzyx", piece, x_mats, precision=highest))
    return jnp.concatenate(pieces, axis=3)


def body(estimate, observed, psf_taps):
    depth, rows, width = estimate.shape
    half = (psf_taps.shape[2] - 1) // 2
    views = lax.axis_size("view")
    recorded = lax.all_to_all(observed, "view", split_axis=3, concat_axis=0, tiled=True)
    taps = lax.all_gather(psf_taps, "view", axis=0, tiled=True)
    cols = width // views
    col_start = lax.axis_index("view") * cols
    current = lax.dynamic_slice_in_dim(estimate, col_start, cols, 2)
    normed = taps / jnp.sum(taps, axis=2, keepdims=True)
    flipped = normed[:, :, ::-1]
    fwd_z = many_bands(normed[:, 0], depth, depth, half)
    back_z = many_bands(flipped[:, 0], depth, depth, half)
    back_y = many_bands(flipped[:, 1], rows + 2 * half, rows, 0)
    fwd_y = many_bands(normed[:, 1], rows + 2 * half, rows, 0)
    for _ in range(ITERS):
        extended = extended_2(current, (("view", 2), ("tile", 1)), half)
        blurred = blur(extended, fwd_z, fwd_y, normed[:, 2], cols)
        ratio = recorded / blurred
        ratio_ext = extended_2(ratio, (("view", 3), ("tile", 2)), half)
        log_corr = jnp.log(blur(ratio_ext, back_z, back_y, flipped[:, 2], cols))
        log_total = jnp.sum(log_corr, axis=0)
        current = current * jnp.exp(log_total / views)
    current = lax.all_gather(current, "view", axis=2, tiled=True)
    return current


def fits(mesh, estimate, psf_taps):
    depth, rows, width = estimate.shape
    tiles = mesh.shape["tile"]
    reach = (psf_taps.shape[2] - 1) // 2
    return (
        mesh.shape["view"] == 2
        and tiles % 2 == 0
        and rows % (32 * tiles) == 0
        and rows // tiles >= 2 * (reach + 1)
        and width % (2 * LANES) == 0
        and 4 * reach <= LANES // 2
        and 2 * reach <= LANES // 4
        and depth % 4 == 0
    )


def solution(mesh):
    placed = (P(None, "tile", None), P("view", None, "tile", None), P("view", None, None))

    def run(estimate, observed, psf_taps):
        quick = fits(mesh, estimate, psf_taps)

        def chosen(*blocks):
            if not quick:
                return body(*blocks)
            return two_view_body(*blocks)

        step = jax.shard_map(
            chosen, mesh=mesh, in_specs=placed, out_specs=P(None, "tile", None), check_vma=False
        )
        return step(estimate, observed, psf_taps)

    return run
```

```python
import jax
import jax.numpy as jnp
from jax import lax
from jax.experimental import pallas as pl
from jax.experimental.pallas import tpu as pltpu
from jax.sharding import PartitionSpec as P


ITERS = 2
LANES = 128
VMEM_BYTES = 24 << 20
BF = jnp.bfloat16
F32 = jnp.float32
VMEM = pl.BlockSpec(memory_space=pltpu.VMEM)
SMEM = pl.BlockSpec(memory_space=pltpu.SMEM)
HBM = pl.BlockSpec(memory_space=pltpu.HBM)


def shaped(shape, dtype=F32):
    return jax.ShapeDtypeStruct(shape, dtype)


def call(kernel, outs, in_specs, out_specs=None, scratch=(), **more):
    return pl.pallas_call(
        kernel, out_shape=outs, in_specs=in_specs,
        out_specs=out_specs or jax.tree.map(lambda _: VMEM, outs), scratch_shapes=scratch,
        compiler_params=pltpu.CompilerParams(vmem_limit_bytes=VMEM_BYTES), **more,
    )


def in_hbm(cells):
    return pltpu.with_memory_space_constraint(cells, pltpu.HBM)


def split(cells):
    high = cells.astype(BF)
    return high, (cells - high.astype(F32)).astype(BF)


def block_at(view, place, blocks):
    at = jnp.where(view == 0, place, blocks - 1 - place)
    return pl.ds(pl.multiple_of(at * LANES, LANES), LANES)


def fold(planes, view, parts):
    piece = LANES // parts
    lane = lax.broadcasted_iota(jnp.int32, planes[0].shape, 1)
    first = jnp.where(view == 0, 0, piece)
    total = None
    for at, plane in enumerate(planes):
        moved = pltpu.roll(plane, lax.rem(first + at * piece, LANES), 1)
        total = moved if total is None else jnp.where(lane >= at * piece, moved, total)
    return total


def unfold(folded, view, parts, at):
    piece = LANES // parts
    first = jnp.where(view == 0, LANES, LANES - piece)
    return pltpu.roll(folded, lax.rem(first - at * piece, LANES), 1)


def pack_window(view, planes_of, depth, own, parts, out_ref):
    for place in range(own):
        for z in range(depth):
            out_ref[place * depth + z] = planes_of(z, place)
    for group in range(depth // parts):
        planes = [planes_of(group * parts + at, own) for at in range(parts)]
        out_ref[own * depth + group] = fold(planes, view, parts)


def unpack_window(view, packed_of, depth, own, parts, store):
    for place in range(own):
        for z in range(depth):
            store(z, place, packed_of(place * depth + z))
    for group in range(depth // parts):
        folded = packed_of(own * depth + group)
        for at in range(parts):
            store(group * parts + at, own, unfold(folded, view, parts, at))


def plane_copies(cells_hbm, cells, sems):
    copies = [
        pltpu.make_async_copy(cells_hbm.at[z], cells.at[z], sems.at[z])
        for z in range(cells.shape[0])
    ]
    for copy in copies:
        copy.start()
    return copies


def pack_pair(view, plane_of, z, depth, own, out):
    for at in (z, z + 1):
        for place in range(own):
            out[place * depth + at] = plane_of(at, place)
    out[own * depth + z // 2] = fold([plane_of(at, own) for at in (z, z + 1)], view, 2)


def near_rows(even, rows):
    near = rows // 2
    at_a = pl.multiple_of(jnp.where(even == 1, near, 0), near)
    at_b = pl.multiple_of(jnp.where(even == 1, 0, near), near)
    return at_a, at_b


def load_kernel(
    meta, est_hbm, obs_hbm, taps_hbm, est, obs, taps, send, theirs_a, theirs_b, near_a, near_b,
    est_sems, obs_sems, taps_sem
):
    depth, rows, width = est.shape
    blocks = width // LANES
    own = blocks // 2
    near = rows // 2
    view = meta[0]
    est_copies = plane_copies(est_hbm, est, est_sems)
    obs_copies = plane_copies(obs_hbm.at[0], obs.at[0], obs_sems)
    taps_copy = pltpu.make_async_copy(taps_hbm, taps, taps_sem)
    taps_copy.start()
    for z in range(0, depth, 2):
        est_copies[z].wait()
        est_copies[z + 1].wait()
        pack_pair(view, lambda at, p: est[at, :, block_at(view, p, blocks)], z, depth, own, send)
    for z in range(0, depth, 2):
        obs_copies[z].wait()
        obs_copies[z + 1].wait()
        for window, outs in ((1 - view, (theirs_a, theirs_b)), (view, (near_a, near_b))):
            for out, start in zip(outs, near_rows(meta[1], rows)):
                pack_pair(
                    window,
                    lambda at, p, window=window, start=start: obs[
                        0, at, pl.ds(start, near), block_at(window, p, blocks)
                    ],
                    z, depth, own, out,
                )
    taps_copy.wait()


def bands_kernel(meta, taps, y_out, own_mats, ext_mats, band):
    length = taps.shape[2]
    reach = (length - 1) // 2
    rows = y_out.shape[2]
    span = 2 * rows
    low = (LANES - reach) // 16 * 16
    high = -(-(2 * LANES + reach) // 16) * 16
    at_before = pl.multiple_of(jnp.where(meta[0] == 0, low, 2 * LANES + low), 16)
    at_after = pl.multiple_of(jnp.where(meta[0] == 0, 2 * LANES, 0), 16)
    lag = (
        lax.broadcasted_iota(jnp.int32, (high - low, LANES), 0)
        + (low - LANES)
        - lax.broadcasted_iota(jnp.int32, (high - low, LANES), 1)
    )
    r_at = lax.broadcasted_iota(jnp.int32, (rows, 3 * span), 0)
    s_at = lax.broadcasted_iota(jnp.int32, (rows, 3 * span), 1)
    y_lag = lax.rem(s_at, span) - r_at - rows // 2
    band[...] = jnp.zeros_like(band)
    kinds = [(view, back) for view in range(2) for back in range(2)]

    def banded(lag, axis):
        bands = [jnp.zeros(lag.shape, F32)] * 4
        for at in range(-reach, reach + 1):
            here = lag == at
            for n, (view, back) in enumerate(kinds):
                tap = taps[axis, view, reach - at if back else reach + at]
                bands[n] = jnp.where(here, tap, bands[n])
        return bands

    piece = 16
    for start in range(0, high - low, piece):
        row = low + start
        for n, cells in enumerate(banded(lag[start : start + piece], 2)):
            for which, part in enumerate(split(cells)):
                if row < LANES:
                    band[n, which, pl.ds(at_before + start, piece)] = part
                elif row < 2 * LANES:
                    band[n, which, row : row + piece] = part
                else:
                    band[n, which, pl.ds(at_after + (row - 2 * LANES), piece)] = part
    for n, (view, back) in enumerate(kinds):
        spread_x(band.at[n], own_mats.at[view, back], ext_mats.at[view, back])
    for start in range(0, rows, piece):
        at = slice(start, start + piece)
        for n, y_band in enumerate(banded(y_lag[at], 1)):
            y_high = y_band.astype(BF).astype(F32)
            y_out[kinds[n][0], kinds[n][1], at] = jnp.where(
                s_at[at] < 2 * span, y_high, y_band - y_high
            ).astype(BF)


def spread_x(band, own_mat, ext_mat):
    own = own_mat.shape[1] // LANES
    for part, which in enumerate((0, 1, 0)):
        for src in range(own + 1):
            at = (part * (own + 1) + src) * LANES
            for dst in range(own):
                if abs(src - dst) <= 1:
                    start = (src - dst + 1) * LANES
                    cells = band[which, start : start + LANES, :]
                else:
                    cells = jnp.zeros((LANES, LANES), BF)
                own_mat[at : at + LANES, dst * LANES : (dst + 1) * LANES] = cells
        for src in range(2):
            at = (part * 2 + src) * LANES
            ext_mat[at : at + LANES, :] = band[which, src * LANES : (src + 1) * LANES, :]


def y_stage(source, bands):
    high, low = split(source)
    return jnp.dot(bands, jnp.concatenate([high, low, high], axis=0), preferred_element_type=F32)


def z_stage(taps, view, back, inner, base, rows, outer):
    depth = inner.shape[0]
    reach = (taps.shape[1] - 1) // 2
    for row in range(0, rows, 8):
        planes = [inner[z, base + row : base + row + 8, :] for z in range(depth)]
        for out in range(depth):
            total = None
            for z in range(depth):
                at = reach + (out - z if back else z - out)
                term = taps[view, at] * planes[z]
                total = term if total is None else total + term
            outer[out, row : row + 8, :] = total


def x_stage(cells, own_mat, ext_mat):
    lead, lanes = cells.shape[:-1], cells.shape[-1]
    high, low = split(cells.reshape(-1, lanes))
    left = jnp.concatenate([high, high, low], axis=1)
    own = jnp.dot(left, own_mat[...], preferred_element_type=F32).reshape(*lead, -1)
    if ext_mat is None:
        return own, None
    at = lanes - 2 * LANES
    left = jnp.concatenate([high[:, at:], high[:, at:], low[:, at:]], axis=1)
    ext = jnp.dot(left, ext_mat[...], preferred_element_type=F32).reshape(*lead, LANES)
    return own, ext


def forward_half(source, half, z_taps, y_bands, own_mats, ext_mats, inner, outer, emit):
    depth = inner.shape[1]
    rows = outer.shape[2]
    both = jnp.concatenate([y_bands[0, 0], y_bands[1, 0]], axis=0)
    for z in range(depth):
        inner[half, z] = y_stage(source(z), both)
    for view in range(2):
        z_stage(z_taps, view, False, inner.at[half], view * rows, rows, outer.at[view])
        emit(view, *x_stage(outer[view], own_mats.at[view, 0], ext_mats.at[view, 0]))


def backward(ratio, view, z_taps, y_bands, own_mats, ext_mats, inner, outer):
    depth = ratio.shape[0]
    rows = outer.shape[2]
    for z in range(depth):
        inner[view, z, :rows, :] = y_stage(ratio[z], y_bands[view, 1])
    z_stage(z_taps, view, True, inner.at[view], 0, rows, outer.at[view])
    ext_mat = None if ext_mats is None else ext_mats.at[view, 1]
    return x_stage(outer[view], own_mats.at[view, 1], ext_mat)


def halo_rows(even, rows):
    near = rows // 2
    at_a = pl.multiple_of(jnp.where(even == 1, rows + near, 0), near)
    at_b = pl.multiple_of(jnp.where(even == 1, 0, rows + near), near)
    return at_a, at_b


def cols(place):
    return slice(place * LANES, (place + 1) * LANES)


def half_forward(meta, below, z_taps, got, parts, mats, field, inner, outer, emit):
    depth, rows = field.shape[0], field.shape[1] // 2
    own = field.shape[2] // LANES - 1
    got_at = pl.multiple_of(jnp.where(below, rows, 0), rows)

    def store(z, place, cells):
        field[z, pl.ds(got_at, rows), cols(place)] = cells

    unpack_window(meta[0], lambda n: got[n], depth, own, parts, store)

    def emit_at(v, own_cells, ext):
        for place in range(own + 1):
            cells = ext if place == own else own_cells[:, :, cols(place)]
            emit(v, got_at, place, cells)

    forward_half(lambda z: field[z], 0, z_taps, *mats, inner, outer, emit_at)


def own_rows(below, rows):
    return pl.ds(pl.multiple_of(jnp.where(below, 0, rows), rows), rows)


def first_kernel(
    meta, z_taps, est, obs_own, got_a, got_b, other_a, other_b, y_bands, own_mats, ext_mats,
    obs, ratio, field, inner, outer
):
    depth, rows, width = est.shape
    own = width // LANES // 2
    view = meta[0]
    near = rows // 2
    for place in range(own + 1):
        field[:, rows : 2 * rows, cols(place)] = est[:, :, block_at(view, place, width // LANES)]
        obs[0, :, near : near + rows, cols(place)] = obs_own[
            0, :, :, block_at(view, place, width // LANES)
        ]
    for other, start in zip((other_a, other_b), near_rows(meta[1], rows)):
        at = pl.ds(pl.multiple_of(start + near, near), near)

        def store_other(z, place, cells, at=at):
            obs[1, z, at, cols(place)] = cells

        unpack_window(view, lambda n, other=other: other[n], depth, own, 2, store_other)
    at_a = pl.multiple_of(jnp.where(meta[1] == 1, 2 * rows, 0), rows)
    at_b = pl.multiple_of(jnp.where(meta[1] == 1, 0, 2 * rows), rows)
    for got, at in ((got_a, at_a), (got_b, at_b)):

        def store(z, place, cells, at=at):
            field[z, pl.ds(at, rows), cols(place)] = cells

        unpack_window(view, lambda n, got=got: got[n], depth, own, 2, store)
    both = jnp.concatenate([y_bands[0, 0], y_bands[1, 0]], axis=0)
    for half in range(2):
        for z in range(depth):
            inner[half, z] = y_stage(field[z, half * rows : half * rows + 2 * rows, :], both)
    for v in range(2):
        for half in range(2):
            z_stage(z_taps, v, False, inner.at[half], v * rows, rows, outer.at[v, half])
        own_cells, ext = x_stage(outer[v], own_mats.at[v, 0], ext_mats.at[v, 0])
        for half in range(2):
            for place in range(own + 1):
                cells = ext[half] if place == own else own_cells[half][:, :, cols(place)]
                for quarter in range(2):
                    part = cells[:, quarter * near : (quarter + 1) * near]
                    at = half * rows + quarter * near
                    at = slice(at, at + near)
                    if half != quarter:
                        part = obs[v, :, at, cols(place)] / part
                    ratio[v, :, at, cols(place)] = part


def complete(meta, which, halo_a, halo_b, obs, ratio_in, ratio):
    depth, rows, lanes = obs.shape[1], obs.shape[2] // 2, obs.shape[3]
    near = rows // 2
    own = lanes // LANES - 1
    for halo, at in zip((halo_a, halo_b), halo_rows(meta[1], rows)):
        known = jnp.where(at == 0, 1 - meta[2], 1 - meta[3]) == 1

        def store(z, place, cells, at=at, known=known):
            obs[which, z, pl.ds(at, near), cols(place)] = cells
            blurred = ratio_in[which, z, pl.ds(at, near), cols(place)]
            ratio[which, z, pl.ds(at, near), cols(place)] = jnp.where(known, cells / blurred, 0.0)

        unpack_window(meta[0], lambda n, halo=halo: halo[n], depth, own, 2, store)


def update_kernel(
    meta, z_taps, est, obs_in, ratio_in, own_a, own_b, far_a, far_b, y_bands, own_mats, ext_mats,
    obs, ratio, current, to_send, inner, outer
):
    depth, _, width = est.shape
    own = width // LANES // 2
    view = meta[0]
    backs = []
    for v, halos in enumerate(((own_a, own_b), (far_a, far_b))):
        complete(meta, v, *halos, obs, ratio_in, ratio)
        backs.append(backward(ratio.at[v], v, z_taps, y_bands, own_mats, ext_mats, inner, outer))
    for place in range(own + 1):
        cells = est[:, :, block_at(view, place, width // LANES)]
        mine, other = [
            back[1] if place == own else back[0][:, :, cols(place)] for back in backs
        ]
        current[:, :, cols(place)] = cells * jnp.sqrt(mine * other)
    pack_window(view, lambda z, p: current[z, :, cols(p)], depth, own, 4, to_send)


def second_half(meta, below, z_taps, current, got, obs, mats, ratio, field, inner, outer):
    rows = current.shape[1]
    field[:, own_rows(below, rows), :] = current[...]
    low = jnp.where(meta[2] == 1, rows // 2, 0)
    high = jnp.where(meta[3] == 1, rows + rows // 2, 2 * rows)
    row = lax.broadcasted_iota(jnp.int32, (rows, LANES), 0)

    def emit(v, at, place, cells):
        inside = ((row + at >= low) & (row + at < high))[None]
        where = (v, slice(None), pl.ds(at, rows), cols(place))
        ratio[where] = jnp.where(inside, obs[where] / cells, 0.0)

    half_forward(meta, below, z_taps, got, 4, mats, field, inner, outer, emit)


def second_a_kernel(
    meta, z_taps, current, got_a, obs, y_bands, own_mats, ext_mats,
    ratio, field, inner, outer
):
    mats = (y_bands, own_mats, ext_mats)
    second_half(
        meta, meta[1] == 1, z_taps, current, got_a, obs, mats, ratio, field, inner, outer
    )


def second_b_kernel(
    meta, z_taps, current, got_b, obs, ratio_in, y_bands, own_mats, ext_mats,
    out, ratio, field, inner, outer
):
    own = current.shape[2] // LANES - 1
    mats = (y_bands, own_mats, ext_mats)
    second_half(
        meta, meta[1] != 1, z_taps, current, got_b, obs, mats, ratio, field, inner, outer
    )
    gains = [
        backward(ratio.at[v], v, z_taps, y_bands, own_mats, None, inner, outer)[0]
        for v in range(2)
    ]
    result = current[:, :, : own * LANES] * jnp.sqrt(gains[0] * gains[1])
    for place in range(own):
        at = jnp.where(meta[0] == 0, place, own - 1 - place)
        out[:, :, pl.ds(pl.multiple_of(at * LANES, LANES), LANES)] = result[:, :, cols(place)]


def copy_planes(cells, out, at, sems):
    width = cells.shape[2]
    copies = [
        pltpu.make_async_copy(cells.at[z], out.at[z, :, pl.ds(at, width)], sems.at[z])
        for z in range(cells.shape[0])
    ]
    for copy in copies:
        copy.start()
    for copy in copies:
        copy.wait()


def place_kernel(meta, half, out, sems):
    width = half.shape[2]
    copy_planes(half, out, pl.multiple_of(meta[0] * width, width), sems)


def paired(cells_a, cells_b):
    count = lax.axis_size("tile")
    pairs_a = [(i, i ^ 1) for i in range(count)]
    pairs_b = []
    for i in range(1, count - 1, 2):
        pairs_b += [(i, i + 1), (i + 1, i)]
    got_b = lax.ppermute(cells_b, "tile", pairs_b)
    got_a = lax.ppermute(cells_a, "tile", pairs_a)
    return got_a, got_b


def two_view_body(estimate, observed, psf_taps):
    depth, rows, width = estimate.shape
    own = width // LANES // 2
    lanes = (own + 1) * LANES
    near = rows // 2
    view = lax.axis_index("view")
    tile = lax.axis_index("tile")
    last = lax.axis_size("tile") - 1
    even = 1 - lax.rem(tile, 2)
    swap = [(0, 1), (1, 0)]
    meta = jnp.stack([view, even, tile == 0, tile == last]).astype(jnp.int32)
    count = own * depth + depth // 2
    count_mid = own * depth + depth // 4
    window = shaped((2, depth, 2 * rows, lanes))

    kinds = jnp.transpose(psf_taps, (1, 0, 2))
    packed = shaped((count, rows, LANES))
    packed_near = shaped((count, near, LANES))
    est, obs_own, own_taps, send, theirs_a, theirs_b, near_a, near_b = call(
        load_kernel,
        [shaped(cells.shape) for cells in (estimate, observed, kinds)]
        + [packed] + [packed_near] * 4,
        [SMEM, HBM, HBM, HBM],
        scratch=[pltpu.SemaphoreType.DMA((depth,))] * 2 + [pltpu.SemaphoreType.DMA],
    )(meta, in_hbm(estimate), in_hbm(observed), in_hbm(kinds))
    got_a, got_b = paired(send, send)
    other_b = lax.ppermute(theirs_b, "view", swap)
    other_a = lax.ppermute(theirs_a, "view", swap)
    other_taps = lax.ppermute(own_taps, "view", swap)
    own_a, own_b = paired(near_a, near_b)

    taps = jnp.concatenate([own_taps, other_taps], axis=1)
    normed = taps / jnp.sum(taps, axis=2, keepdims=True)
    z_taps = normed[0]
    mats = call(
        bands_kernel,
        [
            shaped((2, 2, rows, 6 * rows), BF),
            shaped((2, 2, 3 * lanes, own * LANES), BF),
            shaped((2, 2, 6 * LANES, LANES), BF),
        ],
        [SMEM, SMEM], scratch=[pltpu.VMEM((4, 2, 3 * LANES, LANES), BF)],
    )(meta, normed)
    halo_a, halo_b = paired(other_a, other_b)

    stages = [
        pltpu.VMEM((2, depth, 2 * rows, lanes), F32), pltpu.VMEM((2, depth, rows, lanes), F32),
    ]
    scratch = [pltpu.VMEM((depth, 2 * rows, lanes), F32)] + stages
    obs, ratio = call(
        first_kernel, [window, window], [SMEM, SMEM] + [VMEM] * 9,
        scratch=[
            pltpu.VMEM((depth, 3 * rows, lanes), F32), stages[0],
            pltpu.VMEM((2, 2, depth, rows, lanes), F32),
        ],
    )(meta, z_taps, est, obs_own, got_a, got_b, other_a, other_b, *mats)
    obs, _, current, cur_send = call(
        update_kernel,
        [window, window, shaped((depth, rows, lanes)), shaped((count_mid, rows, LANES))],
        [SMEM, SMEM] + [VMEM] * 10, scratch=stages, input_output_aliases={3: 0, 4: 1},
    )(meta, z_taps, est, obs, ratio, own_a, own_b, halo_a, halo_b, *mats)
    cur_a, cur_b = paired(cur_send, cur_send)
    ratio = call(
        second_a_kernel, window, [SMEM, SMEM] + [VMEM] * 6, scratch=scratch
    )(meta, z_taps, current, cur_a, obs, *mats)
    half, _ = call(
        second_b_kernel, [shaped((depth, rows, own * LANES)), window],
        [SMEM, SMEM] + [VMEM] * 7, scratch=scratch, input_output_aliases={5: 1},
    )(meta, z_taps, current, cur_b, obs, ratio, *mats)
    far = lax.ppermute(half, "view", swap)
    partial = call(
        place_kernel, shaped(estimate.shape), [SMEM, VMEM], HBM,
        scratch=[pltpu.SemaphoreType.DMA((depth,))],
    )(meta, half)
    return lax.dynamic_update_slice(partial, far, (0, 0, (1 - view) * own * LANES))


def extended_2(cells, sides, width):
    for axis, dim in sides:
        count = lax.axis_size(axis)
        ends = count - 1
        head = lax.slice_in_dim(cells, 0, width, axis=dim)
        tail = lax.slice_in_dim(cells, cells.shape[dim] - width, cells.shape[dim], axis=dim)
        cells = jnp.concatenate(
            [
                lax.ppermute(tail, axis, [(i, (i + 1) % count) for i in range(ends)]),
                cells,
                lax.ppermute(head, axis, [((i + 1) % count, i) for i in range(ends)]),
            ],
            axis=dim,
        )
    return cells


def band_matrix(taps, count_in, count_out, offset):
    rows_in = jnp.arange(count_in)[:, None]
    cols_out = jnp.arange(count_out)[None, :]
    lag = rows_in - cols_out + offset
    length = taps.shape[0]
    inside = (lag >= 0) & (lag < length)
    return jnp.where(inside, jnp.take(taps, jnp.clip(lag, 0, length - 1)), 0.0)


def many_bands(taps, count_in, count_out, offset):
    return jax.vmap(lambda one: band_matrix(one, count_in, count_out, offset))(taps)


def blur(field, z_mats, y_mats, x_taps, cols_out):
    highest = lax.Precision.HIGHEST
    if field.ndim == 3:
        out = jnp.einsum("kyx,vkz->vzyx", field, z_mats, precision=highest)
    else:
        out = jnp.einsum("vkyx,vkz->vzyx", field, z_mats, precision=highest)
    out = jnp.einsum("vzjx,vjy->vzyx", out, y_mats, precision=highest)
    reach = (x_taps.shape[1] - 1) // 2
    pieces = []
    for start in range(0, cols_out, 128):
        block = min(128, cols_out - start)
        x_mats = many_bands(x_taps, block + 2 * reach, block, 0)
        piece = lax.slice_in_dim(out, start, start + block + 2 * reach, axis=3)
        pieces.append(jnp.einsum("vzyj,vjx->vzyx", piece, x_mats, precision=highest))
    return jnp.concatenate(pieces, axis=3)


def body(estimate, observed, psf_taps):
    depth, rows, width = estimate.shape
    half = (psf_taps.shape[2] - 1) // 2
    views = lax.axis_size("view")
    recorded = lax.all_to_all(observed, "view", split_axis=3, concat_axis=0, tiled=True)
    taps = lax.all_gather(psf_taps, "view", axis=0, tiled=True)
    cols = width // views
    col_start = lax.axis_index("view") * cols
    current = lax.dynamic_slice_in_dim(estimate, col_start, cols, 2)
    normed = taps / jnp.sum(taps, axis=2, keepdims=True)
    flipped = normed[:, :, ::-1]
    fwd_z = many_bands(normed[:, 0], depth, depth, half)
    back_z = many_bands(flipped[:, 0], depth, depth, half)
    back_y = many_bands(flipped[:, 1], rows + 2 * half, rows, 0)
    fwd_y = many_bands(normed[:, 1], rows + 2 * half, rows, 0)
    for _ in range(ITERS):
        extended = extended_2(current, (("view", 2), ("tile", 1)), half)
        blurred = blur(extended, fwd_z, fwd_y, normed[:, 2], cols)
        ratio = recorded / blurred
        ratio_ext = extended_2(ratio, (("view", 3), ("tile", 2)), half)
        log_corr = jnp.log(blur(ratio_ext, back_z, back_y, flipped[:, 2], cols))
        log_total = jnp.sum(log_corr, axis=0)
        current = current * jnp.exp(log_total / views)
    current = lax.all_gather(current, "view", axis=2, tiled=True)
    return current


def fits(mesh, estimate, psf_taps):
    depth, rows, width = estimate.shape
    tiles = mesh.shape["tile"]
    reach = (psf_taps.shape[2] - 1) // 2
    return (
        mesh.shape["view"] == 2
        and tiles % 2 == 0
        and rows % (32 * tiles) == 0
        and rows // tiles >= 2 * (reach + 1)
        and width % (2 * LANES) == 0
        and 4 * reach <= LANES // 2
        and 2 * reach <= LANES // 4
        and depth % 4 == 0
    )


def solution(mesh):
    placed = (P(None, "tile", None), P("view", None, "tile", None), P("view", None, None))


    def run(estimate, observed, psf_taps):
        quick = fits(mesh, estimate, psf_taps)

        def chosen(*blocks):
            if not quick:
                return body(*blocks)
            return two_view_body(*blocks)

        step = jax.shard_map(
            chosen, mesh=mesh, in_specs=placed, out_specs=P(None, "tile", None), check_vma=False
        )
        return step(estimate, observed, psf_taps)

    return run
```

```python
import jax
import jax.numpy as jnp
from jax import lax
from jax.experimental import pallas as pl
from jax.experimental.pallas import tpu as pltpu
from jax.sharding import PartitionSpec as P


ITERS = 2
LANES = 128
VMEM_BYTES = 24 << 20
BF = jnp.bfloat16
F32 = jnp.float32
VMEM = pl.BlockSpec(memory_space=pltpu.VMEM)
SMEM = pl.BlockSpec(memory_space=pltpu.SMEM)
HBM = pl.BlockSpec(memory_space=pltpu.HBM)


def shaped(shape, dtype=F32):
    return jax.ShapeDtypeStruct(shape, dtype)


def call(kernel, outs, in_specs, out_specs=None, scratch=(), **more):
    return pl.pallas_call(
        kernel, out_shape=outs, in_specs=in_specs,
        out_specs=out_specs or jax.tree.map(lambda _: VMEM, outs), scratch_shapes=scratch,
        compiler_params=pltpu.CompilerParams(vmem_limit_bytes=VMEM_BYTES), **more,
    )


def in_hbm(cells):
    return pltpu.with_memory_space_constraint(cells, pltpu.HBM)


def split(cells):
    high = cells.astype(BF)
    return high, (cells - high.astype(F32)).astype(BF)


def block_at(view, place, blocks):
    at = jnp.where(view == 0, place, blocks - 1 - place)
    return pl.ds(pl.multiple_of(at * LANES, LANES), LANES)


def fold(planes, view, parts):
    piece = LANES // parts
    lane = lax.broadcasted_iota(jnp.int32, planes[0].shape, 1)
    first = jnp.where(view == 0, 0, piece)
    total = None
    for at, plane in enumerate(planes):
        moved = pltpu.roll(plane, lax.rem(first + at * piece, LANES), 1)
        total = moved if total is None else jnp.where(lane >= at * piece, moved, total)
    return total


def unfold(folded, view, parts, at):
    piece = LANES // parts
    first = jnp.where(view == 0, LANES, LANES - piece)
    return pltpu.roll(folded, lax.rem(first - at * piece, LANES), 1)


def pack_window(view, planes_of, depth, own, parts, out_ref):
    for place in range(own):
        for z in range(depth):
            out_ref[place * depth + z] = planes_of(z, place)
    for group in range(depth // parts):
        planes = [planes_of(group * parts + at, own) for at in range(parts)]
        out_ref[own * depth + group] = fold(planes, view, parts)


def unpack_window(view, packed_of, depth, own, parts, store):
    for place in range(own):
        for z in range(depth):
            store(z, place, packed_of(place * depth + z))
    for group in range(depth // parts):
        folded = packed_of(own * depth + group)
        for at in range(parts):
            store(group * parts + at, own, unfold(folded, view, parts, at))


def plane_copies(cells_hbm, cells, sems):
    copies = [
        pltpu.make_async_copy(cells_hbm.at[z], cells.at[z], sems.at[z])
        for z in range(cells.shape[0])
    ]
    for copy in copies:
        copy.start()
    return copies


def pack_pair(view, plane_of, z, depth, own, out):
    for at in (z, z + 1):
        for place in range(own):
            out[place * depth + at] = plane_of(at, place)
    out[own * depth + z // 2] = fold([plane_of(at, own) for at in (z, z + 1)], view, 2)


def near_rows(even, rows):
    near = rows // 2
    at_a = pl.multiple_of(jnp.where(even == 1, near, 0), near)
    at_b = pl.multiple_of(jnp.where(even == 1, 0, near), near)
    return at_a, at_b


def load_kernel(
    meta, est_hbm, obs_hbm, taps_hbm, est, obs, taps, send, theirs_a, theirs_b, near_a, near_b,
    est_sems, obs_sems, taps_sem
):
    depth, rows, width = est.shape
    blocks = width // LANES
    own = blocks // 2
    near = rows // 2
    view = meta[0]
    est_copies = plane_copies(est_hbm, est, est_sems)
    obs_copies = plane_copies(obs_hbm.at[0], obs.at[0], obs_sems)
    taps_copy = pltpu.make_async_copy(taps_hbm, taps, taps_sem)
    taps_copy.start()
    for z in range(0, depth, 2):
        est_copies[z].wait()
        est_copies[z + 1].wait()
        pack_pair(view, lambda at, p: est[at, :, block_at(view, p, blocks)], z, depth, own, send)
    for z in range(0, depth, 2):
        obs_copies[z].wait()
        obs_copies[z + 1].wait()
        for window, outs in ((1 - view, (theirs_a, theirs_b)), (view, (near_a, near_b))):
            for out, start in zip(outs, near_rows(meta[1], rows)):
                pack_pair(
                    window,
                    lambda at, p, window=window, start=start: obs[
                        0, at, pl.ds(start, near), block_at(window, p, blocks)
                    ],
                    z, depth, own, out,
                )
    taps_copy.wait()


def bands_kernel(meta, taps, y_out, own_mats, ext_mats, band):
    length = taps.shape[2]
    reach = (length - 1) // 2
    rows = y_out.shape[2]
    span = 2 * rows
    low = (LANES - reach) // 16 * 16
    high = -(-(2 * LANES + reach) // 16) * 16
    at_before = pl.multiple_of(jnp.where(meta[0] == 0, low, 2 * LANES + low), 16)
    at_after = pl.multiple_of(jnp.where(meta[0] == 0, 2 * LANES, 0), 16)
    lag = (
        lax.broadcasted_iota(jnp.int32, (high - low, LANES), 0)
        + (low - LANES)
        - lax.broadcasted_iota(jnp.int32, (high - low, LANES), 1)
    )
    r_at = lax.broadcasted_iota(jnp.int32, (rows, 3 * span), 0)
    s_at = lax.broadcasted_iota(jnp.int32, (rows, 3 * span), 1)
    y_lag = lax.rem(s_at, span) - r_at - rows // 2
    band[...] = jnp.zeros_like(band)
    kinds = [(view, back) for view in range(2) for back in range(2)]

    def banded(lag, axis):
        bands = [jnp.zeros(lag.shape, F32)] * 4
        for at in range(-reach, reach + 1):
            here = lag == at
            for n, (view, back) in enumerate(kinds):
                tap = taps[axis, view, reach - at if back else reach + at]
                bands[n] = jnp.where(here, tap, bands[n])
        return bands

    piece = 16
    for start in range(0, high - low, piece):
        row = low + start
        for n, cells in enumerate(banded(lag[start : start + piece], 2)):
            for which, part in enumerate(split(cells)):
                if row < LANES:
                    band[n, which, pl.ds(at_before + start, piece)] = part
                elif row < 2 * LANES:
                    band[n, which, row : row + piece] = part
                else:
                    band[n, which, pl.ds(at_after + (row - 2 * LANES), piece)] = part
    for n, (view, back) in enumerate(kinds):
        spread_x(band.at[n], own_mats.at[view, back], ext_mats.at[view, back])
    for start in range(0, rows, piece):
        at = slice(start, start + piece)
        for n, y_band in enumerate(banded(y_lag[at], 1)):
            y_high = y_band.astype(BF).astype(F32)
            y_out[kinds[n][0], kinds[n][1], at] = jnp.where(
                s_at[at] < 2 * span, y_high, y_band - y_high
            ).astype(BF)


def spread_x(band, own_mat, ext_mat):
    own = own_mat.shape[1] // LANES
    for part, which in enumerate((0, 1, 0)):
        for src in range(own + 1):
            at = (part * (own + 1) + src) * LANES
            for dst in range(own):
                if abs(src - dst) <= 1:
                    start = (src - dst + 1) * LANES
                    cells = band[which, start : start + LANES, :]
                else:
                    cells = jnp.zeros((LANES, LANES), BF)
                own_mat[at : at + LANES, dst * LANES : (dst + 1) * LANES] = cells
        for src in range(2):
            at = (part * 2 + src) * LANES
            ext_mat[at : at + LANES, :] = band[which, src * LANES : (src + 1) * LANES, :]


def y_stage(source, bands):
    high, low = split(source)
    return jnp.dot(bands, jnp.concatenate([high, low, high], axis=0), preferred_element_type=F32)


def z_stage(taps, view, back, inner, base, rows, outer, outs=None):
    depth = inner.shape[0]
    outs = range(depth) if outs is None else outs
    reach = (taps.shape[1] - 1) // 2
    for row in range(0, rows, 8):
        planes = [inner[z, base + row : base + row + 8, :] for z in range(depth)]
        for out in outs:
            total = None
            for z in range(depth):
                at = reach + (out - z if back else z - out)
                term = taps[view, at] * planes[z]
                total = term if total is None else total + term
            outer[out - outs[0], row : row + 8, :] = total


def x_stage(cells, own_mat, ext_mat):
    lead, lanes = cells.shape[:-1], cells.shape[-1]
    high, low = split(cells.reshape(-1, lanes))
    left = jnp.concatenate([high, high, low], axis=1)
    own = jnp.dot(left, own_mat[...], preferred_element_type=F32).reshape(*lead, -1)
    if ext_mat is None:
        return own, None
    at = lanes - 2 * LANES
    left = jnp.concatenate([high[:, at:], high[:, at:], low[:, at:]], axis=1)
    ext = jnp.dot(left, ext_mat[...], preferred_element_type=F32).reshape(*lead, LANES)
    return own, ext


def forward_half(source, half, z_taps, y_bands, own_mats, ext_mats, inner, outer, emit):
    depth = inner.shape[1]
    rows = outer.shape[2]
    both = jnp.concatenate([y_bands[0, 0], y_bands[1, 0]], axis=0)
    for z in range(depth):
        inner[half, z] = y_stage(source(z), both)
    for view in range(2):
        z_stage(z_taps, view, False, inner.at[half], view * rows, rows, outer.at[view])
        emit(view, *x_stage(outer[view], own_mats.at[view, 0], ext_mats.at[view, 0]))


def backward(ratio, view, z_taps, y_bands, own_mats, ext_mats, inner, outer):
    depth = ratio.shape[0]
    rows = outer.shape[2]
    for z in range(depth):
        inner[view, z, :rows, :] = y_stage(ratio[z], y_bands[view, 1])
    z_stage(z_taps, view, True, inner.at[view], 0, rows, outer.at[view])
    ext_mat = None if ext_mats is None else ext_mats.at[view, 1]
    return x_stage(outer[view], own_mats.at[view, 1], ext_mat)


def halo_rows(even, rows):
    near = rows // 2
    at_a = pl.multiple_of(jnp.where(even == 1, rows + near, 0), near)
    at_b = pl.multiple_of(jnp.where(even == 1, 0, rows + near), near)
    return at_a, at_b


def cols(place):
    return slice(place * LANES, (place + 1) * LANES)


def half_forward(meta, below, z_taps, got, parts, mats, field, inner, outer, emit):
    depth, rows = field.shape[0], field.shape[1] // 2
    own = field.shape[2] // LANES - 1
    got_at = pl.multiple_of(jnp.where(below, rows, 0), rows)

    def store(z, place, cells):
        field[z, pl.ds(got_at, rows), cols(place)] = cells

    unpack_window(meta[0], lambda n: got[n], depth, own, parts, store)

    def emit_at(v, own_cells, ext):
        for place in range(own + 1):
            cells = ext if place == own else own_cells[:, :, cols(place)]
            emit(v, got_at, place, cells)

    forward_half(lambda z: field[z], 0, z_taps, *mats, inner, outer, emit_at)


def own_rows(below, rows):
    return pl.ds(pl.multiple_of(jnp.where(below, 0, rows), rows), rows)


def first_kernel(
    meta, z_taps, est, obs_own, got_a, got_b, other_a, other_b, y_bands, own_mats, ext_mats,
    obs, ratio, field, inner, outer
):
    depth, rows, width = est.shape
    own = width // LANES // 2
    view = meta[0]
    near = rows // 2
    for place in range(own + 1):
        field[:, rows : 2 * rows, cols(place)] = est[:, :, block_at(view, place, width // LANES)]
        obs[0, :, near : near + rows, cols(place)] = obs_own[
            0, :, :, block_at(view, place, width // LANES)
        ]
    for other, start in zip((other_a, other_b), near_rows(meta[1], rows)):
        at = pl.ds(pl.multiple_of(start + near, near), near)

        def store_other(z, place, cells, at=at):
            obs[1, z, at, cols(place)] = cells

        unpack_window(view, lambda n, other=other: other[n], depth, own, 2, store_other)
    at_a = pl.multiple_of(jnp.where(meta[1] == 1, 2 * rows, 0), rows)
    at_b = pl.multiple_of(jnp.where(meta[1] == 1, 0, 2 * rows), rows)
    for got, at in ((got_a, at_a), (got_b, at_b)):

        def store(z, place, cells, at=at):
            field[z, pl.ds(at, rows), cols(place)] = cells

        unpack_window(view, lambda n, got=got: got[n], depth, own, 2, store)
    both = jnp.concatenate([y_bands[0, 0], y_bands[1, 0]], axis=0)
    for half in range(2):
        for z in range(depth):
            inner[half, z] = y_stage(field[z, half * rows : half * rows + 2 * rows, :], both)
    for v in range(2):
        for half in range(2):
            z_stage(z_taps, v, False, inner.at[half], v * rows, rows, outer.at[v, half])
        own_cells, ext = x_stage(outer[v], own_mats.at[v, 0], ext_mats.at[v, 0])
        for half in range(2):
            for place in range(own + 1):
                cells = ext[half] if place == own else own_cells[half][:, :, cols(place)]
                for quarter in range(2):
                    part = cells[:, quarter * near : (quarter + 1) * near]
                    at = half * rows + quarter * near
                    at = slice(at, at + near)
                    if half != quarter:
                        part = obs[v, :, at, cols(place)] / part
                    ratio[v, :, at, cols(place)] = part


def complete(meta, which, halo_a, halo_b, obs, ratio_in, ratio):
    depth, rows, lanes = obs.shape[1], obs.shape[2] // 2, obs.shape[3]
    near = rows // 2
    own = lanes // LANES - 1
    for halo, at in zip((halo_a, halo_b), halo_rows(meta[1], rows)):
        known = jnp.where(at == 0, 1 - meta[2], 1 - meta[3]) == 1

        def store(z, place, cells, at=at, known=known):
            obs[which, z, pl.ds(at, near), cols(place)] = cells
            blurred = ratio_in[which, z, pl.ds(at, near), cols(place)]
            ratio[which, z, pl.ds(at, near), cols(place)] = jnp.where(known, cells / blurred, 0.0)

        unpack_window(meta[0], lambda n, halo=halo: halo[n], depth, own, 2, store)


def update_kernel(
    meta, z_taps, est, obs_in, ratio_in, own_a, own_b, far_a, far_b, y_bands, own_mats, ext_mats,
    obs, ratio, current, to_send, inner, outer
):
    depth, _, width = est.shape
    own = width // LANES // 2
    view = meta[0]
    backs = []
    for v, halos in enumerate(((own_a, own_b), (far_a, far_b))):
        complete(meta, v, *halos, obs, ratio_in, ratio)
        backs.append(backward(ratio.at[v], v, z_taps, y_bands, own_mats, ext_mats, inner, outer))
    for place in range(own + 1):
        cells = est[:, :, block_at(view, place, width // LANES)]
        mine, other = [
            back[1] if place == own else back[0][:, :, cols(place)] for back in backs
        ]
        current[:, :, cols(place)] = cells * jnp.sqrt(mine * other)
    pack_window(view, lambda z, p: current[z, :, cols(p)], depth, own, 4, to_send)


def second_half(meta, below, z_taps, current, got, obs, mats, ratio, field, inner, outer):
    rows = current.shape[1]
    field[:, own_rows(below, rows), :] = current[...]
    low = jnp.where(meta[2] == 1, rows // 2, 0)
    high = jnp.where(meta[3] == 1, rows + rows // 2, 2 * rows)
    row = lax.broadcasted_iota(jnp.int32, (rows, LANES), 0)

    def emit(v, at, place, cells):
        inside = ((row + at >= low) & (row + at < high))[None]
        where = (v, slice(None), pl.ds(at, rows), cols(place))
        ratio[where] = jnp.where(inside, obs[where] / cells, 0.0)

    half_forward(meta, below, z_taps, got, 4, mats, field, inner, outer, emit)


def second_a_kernel(
    meta, z_taps, current, got_a, obs, y_bands, own_mats, ext_mats,
    ratio, field, inner, outer
):
    mats = (y_bands, own_mats, ext_mats)
    second_half(
        meta, meta[1] == 1, z_taps, current, got_a, obs, mats, ratio, field, inner, outer
    )


def finish(meta, z_taps, current, inner, own_mats, outer, planes, out):
    own = current.shape[2] // LANES - 1
    gains = []
    for v in range(2):
        z_stage(z_taps, v, True, inner.at[v], 0, inner.shape[2], outer.at[v], planes)
        gains.append(x_stage(outer[v, : len(planes)], own_mats.at[v, 1], None)[0])
    kept = current[planes[0] : planes[-1] + 1, :, : own * LANES]
    result = kept * jnp.sqrt(gains[0] * gains[1])
    for place in range(own):
        at = jnp.where(meta[0] == 0, place, own - 1 - place)
        out[:, :, pl.ds(pl.multiple_of(at * LANES, LANES), LANES)] = result[:, :, cols(place)]


def second_b_kernel(
    meta, z_taps, current, got_b, obs, ratio_in, y_bands, own_mats, ext_mats,
    out, ratio, after_y, field, inner, outer
):
    depth = current.shape[0]
    mats = (y_bands, own_mats, ext_mats)
    second_half(
        meta, meta[1] != 1, z_taps, current, got_b, obs, mats, ratio, field, inner, outer
    )
    for v in range(2):
        for z in range(depth):
            after_y[v, z] = y_stage(ratio[v, z], y_bands[v, 1])
    finish(meta, z_taps, current, after_y, own_mats, outer, range(depth // 2), out)


def second_c_kernel(meta, z_taps, current, after_y, own_mats, out, outer):
    depth = current.shape[0]
    finish(meta, z_taps, current, after_y, own_mats, outer, range(depth // 2, depth), out)


def place_kernel(meta, first, second, out, sems):
    width = first.shape[2]
    at = pl.multiple_of(meta[0] * width, width)
    planes = [first.at[z] for z in range(first.shape[0])]
    planes += [second.at[z] for z in range(second.shape[0])]
    copies = [
        pltpu.make_async_copy(plane, out.at[z, :, pl.ds(at, width)], sems.at[z])
        for z, plane in enumerate(planes)
    ]
    for copy in copies:
        copy.start()
    for copy in copies:
        copy.wait()


def paired(cells_a, cells_b):
    count = lax.axis_size("tile")
    pairs_a = [(i, i ^ 1) for i in range(count)]
    pairs_b = []
    for i in range(1, count - 1, 2):
        pairs_b += [(i, i + 1), (i + 1, i)]
    got_b = lax.ppermute(cells_b, "tile", pairs_b)
    got_a = lax.ppermute(cells_a, "tile", pairs_a)
    return got_a, got_b


def two_view_body(estimate, observed, psf_taps):
    depth, rows, width = estimate.shape
    own = width // LANES // 2
    lanes = (own + 1) * LANES
    near = rows // 2
    view = lax.axis_index("view")
    tile = lax.axis_index("tile")
    last = lax.axis_size("tile") - 1
    even = 1 - lax.rem(tile, 2)
    swap = [(0, 1), (1, 0)]
    meta = jnp.stack([view, even, tile == 0, tile == last]).astype(jnp.int32)
    count = own * depth + depth // 2
    count_mid = own * depth + depth // 4
    window = shaped((2, depth, 2 * rows, lanes))

    kinds = jnp.transpose(psf_taps, (1, 0, 2))
    packed = shaped((count, rows, LANES))
    packed_near = shaped((count, near, LANES))
    est, obs_own, own_taps, send, theirs_a, theirs_b, near_a, near_b = call(
        load_kernel,
        [shaped(cells.shape) for cells in (estimate, observed, kinds)]
        + [packed] + [packed_near] * 4,
        [SMEM, HBM, HBM, HBM],
        scratch=[pltpu.SemaphoreType.DMA((depth,))] * 2 + [pltpu.SemaphoreType.DMA],
    )(meta, in_hbm(estimate), in_hbm(observed), in_hbm(kinds))
    got_a, got_b = paired(send, send)
    other_b = lax.ppermute(theirs_b, "view", swap)
    other_a = lax.ppermute(theirs_a, "view", swap)
    other_taps = lax.ppermute(own_taps, "view", swap)
    own_a, own_b = paired(near_a, near_b)

    taps = jnp.concatenate([own_taps, other_taps], axis=1)
    normed = taps / jnp.sum(taps, axis=2, keepdims=True)
    z_taps = normed[0]
    mats = call(
        bands_kernel,
        [
            shaped((2, 2, rows, 6 * rows), BF),
            shaped((2, 2, 3 * lanes, own * LANES), BF),
            shaped((2, 2, 6 * LANES, LANES), BF),
        ],
        [SMEM, SMEM], scratch=[pltpu.VMEM((4, 2, 3 * LANES, LANES), BF)],
    )(meta, normed)
    halo_a, halo_b = paired(other_a, other_b)

    stages = [
        pltpu.VMEM((2, depth, 2 * rows, lanes), F32), pltpu.VMEM((2, depth, rows, lanes), F32),
    ]
    scratch = [pltpu.VMEM((depth, 2 * rows, lanes), F32)] + stages
    obs, ratio = call(
        first_kernel, [window, window], [SMEM, SMEM] + [VMEM] * 9,
        scratch=[
            pltpu.VMEM((depth, 3 * rows, lanes), F32), stages[0],
            pltpu.VMEM((2, 2, depth, rows, lanes), F32),
        ],
    )(meta, z_taps, est, obs_own, got_a, got_b, other_a, other_b, *mats)
    obs, _, current, cur_send = call(
        update_kernel,
        [window, window, shaped((depth, rows, lanes)), shaped((count_mid, rows, LANES))],
        [SMEM, SMEM] + [VMEM] * 10, scratch=stages, input_output_aliases={3: 0, 4: 1},
    )(meta, z_taps, est, obs, ratio, own_a, own_b, halo_a, halo_b, *mats)
    cur_a, cur_b = paired(cur_send, cur_send)
    ratio = call(
        second_a_kernel, window, [SMEM, SMEM] + [VMEM] * 6, scratch=scratch
    )(meta, z_taps, current, cur_a, obs, *mats)
    part = shaped((depth // 2, rows, own * LANES))
    half_0, _, after_y = call(
        second_b_kernel, [part, window, shaped((2, depth, rows, lanes))],
        [SMEM, SMEM] + [VMEM] * 7, scratch=scratch, input_output_aliases={5: 1},
    )(meta, z_taps, current, cur_b, obs, ratio, *mats)
    far_0 = lax.ppermute(half_0, "view", swap)
    half_1 = call(
        second_c_kernel, part, [SMEM, SMEM] + [VMEM] * 3, scratch=stages[1:],
    )(meta, z_taps, current, after_y, mats[1])
    far_1 = lax.ppermute(half_1, "view", swap)
    out = call(
        place_kernel, shaped(estimate.shape), [SMEM, VMEM, VMEM], HBM,
        scratch=[pltpu.SemaphoreType.DMA((depth,))],
    )(meta, half_0, half_1)
    at = (1 - view) * own * LANES
    out = lax.dynamic_update_slice(out, far_0, (0, 0, at))
    return lax.dynamic_update_slice(out, far_1, (depth // 2, 0, at))


def extended_2(cells, sides, width):
    for axis, dim in sides:
        count = lax.axis_size(axis)
        ends = count - 1
        head = lax.slice_in_dim(cells, 0, width, axis=dim)
        tail = lax.slice_in_dim(cells, cells.shape[dim] - width, cells.shape[dim], axis=dim)
        cells = jnp.concatenate(
            [
                lax.ppermute(tail, axis, [(i, (i + 1) % count) for i in range(ends)]),
                cells,
                lax.ppermute(head, axis, [((i + 1) % count, i) for i in range(ends)]),
            ],
            axis=dim,
        )
    return cells


def band_matrix(taps, count_in, count_out, offset):
    rows_in = jnp.arange(count_in)[:, None]
    cols_out = jnp.arange(count_out)[None, :]
    lag = rows_in - cols_out + offset
    length = taps.shape[0]
    inside = (lag >= 0) & (lag < length)
    return jnp.where(inside, jnp.take(taps, jnp.clip(lag, 0, length - 1)), 0.0)


def many_bands(taps, count_in, count_out, offset):
    return jax.vmap(lambda one: band_matrix(one, count_in, count_out, offset))(taps)


def blur(field, z_mats, y_mats, x_taps, cols_out):
    highest = lax.Precision.HIGHEST
    if field.ndim == 3:
        out = jnp.einsum("kyx,vkz->vzyx", field, z_mats, precision=highest)
    else:
        out = jnp.einsum("vkyx,vkz->vzyx", field, z_mats, precision=highest)
    out = jnp.einsum("vzjx,vjy->vzyx", out, y_mats, precision=highest)
    reach = (x_taps.shape[1] - 1) // 2
    pieces = []
    for start in range(0, cols_out, 128):
        block = min(128, cols_out - start)
        x_mats = many_bands(x_taps, block + 2 * reach, block, 0)
        piece = lax.slice_in_dim(out, start, start + block + 2 * reach, axis=3)
        pieces.append(jnp.einsum("vzyj,vjx->vzyx", piece, x_mats, precision=highest))
    return jnp.concatenate(pieces, axis=3)


def body(estimate, observed, psf_taps):
    depth, rows, width = estimate.shape
    half = (psf_taps.shape[2] - 1) // 2
    views = lax.axis_size("view")
    recorded = lax.all_to_all(observed, "view", split_axis=3, concat_axis=0, tiled=True)
    taps = lax.all_gather(psf_taps, "view", axis=0, tiled=True)
    cols = width // views
    col_start = lax.axis_index("view") * cols
    current = lax.dynamic_slice_in_dim(estimate, col_start, cols, 2)
    normed = taps / jnp.sum(taps, axis=2, keepdims=True)
    flipped = normed[:, :, ::-1]
    fwd_z = many_bands(normed[:, 0], depth, depth, half)
    back_z = many_bands(flipped[:, 0], depth, depth, half)
    back_y = many_bands(flipped[:, 1], rows + 2 * half, rows, 0)
    fwd_y = many_bands(normed[:, 1], rows + 2 * half, rows, 0)
    for _ in range(ITERS):
        extended = extended_2(current, (("view", 2), ("tile", 1)), half)
        blurred = blur(extended, fwd_z, fwd_y, normed[:, 2], cols)
        ratio = recorded / blurred
        ratio_ext = extended_2(ratio, (("view", 3), ("tile", 2)), half)
        log_corr = jnp.log(blur(ratio_ext, back_z, back_y, flipped[:, 2], cols))
        log_total = jnp.sum(log_corr, axis=0)
        current = current * jnp.exp(log_total / views)
    current = lax.all_gather(current, "view", axis=2, tiled=True)
    return current


def fits(mesh, estimate, psf_taps):
    depth, rows, width = estimate.shape
    tiles = mesh.shape["tile"]
    reach = (psf_taps.shape[2] - 1) // 2
    return (
        mesh.shape["view"] == 2
        and tiles % 2 == 0
        and rows % (32 * tiles) == 0
        and rows // tiles >= 2 * (reach + 1)
        and width % (2 * LANES) == 0
        and 4 * reach <= LANES // 2
        and 2 * reach <= LANES // 4
        and depth % 4 == 0
    )


def solution(mesh):
    placed = (P(None, "tile", None), P("view", None, "tile", None), P("view", None, None))


    def run(estimate, observed, psf_taps):
        quick = fits(mesh, estimate, psf_taps)

        def chosen(*blocks):
            if not quick:
                return body(*blocks)
            return two_view_body(*blocks)

        step = jax.shard_map(
            chosen, mesh=mesh, in_specs=placed, out_specs=P(None, "tile", None), check_vma=False
        )
        return step(estimate, observed, psf_taps)

    return run
```
